256 devices in a mesh: group: 8 (over z), dev: 32 (over x, y, core).
Axes of the slice: x: 4, y: 4, z: 8, core: 2. Of those that a mesh axis runs over, the one named last changes fastest.
Arguments:
- corpus_tokens: bfloat16 [32768, 1024], P(('group', 'dev')), may hold values from -6 to 6
- norm_gain: float32 [1024], replicated, may hold values from 0.1 to 1.9
- wi_weight: bfloat16 [1024, 5248], P('dev'), may hold values from -0.1875 to 0.1875
- wo_weight: bfloat16 [2624, 1024], P('dev'), may hold values from -0.125 to 0.125
- final_gain: float32 [1024], replicated, may hold values from 0.1 to 1.9
- proj_weight: bfloat16 [1024, 128], replicated, may hold values from -0.1875 to 0.1875
- query_vectors: bfloat16 [512, 32, 128], P(('group', 'dev')), may hold values from -6 to 6
- doc_lengths: int32 [8, 16], P('group'), may hold values from 1 to 2048, 4096 in all within a row
- candidates: int32 [512, 100], P(('group', 'dev')), may hold values from 0 to 127
Outputs:
- doc_vectors: bfloat16 [32768, 128], P(('group', 'dev'))
- scores: float32 [512, 100], P(('group', 'dev'))
The draws below stay inside these ranges and needn't reach their ends.
Inputs may be any that keep to these rules, and one draw needn't show every extreme that they name: `doc_lengths`: each row sums to 4096; its largest length is exactly 2048. `candidates`: document k of group g has id g * 16 + k; ids may repeat within a row.
All inputs are finite; a program needn't handle non-finite values.
Results may differ from the reference program's by a relative error of at most 0.0062.
Values may be sent and summed in bfloat16 or wider, within the bound.
A program may use at most 128 MiB of HBM per device.

```python
import math
import jax
import jax.numpy as jnp
import numpy as np
from jax import lax

D = 1024
FF = 2624
DIM = 128
QT = 32
NCAND = 100
DOCS_G = 16
SHARD = 4096
DOC_MOST = 2048
TOKENS = 32768
NDOCS = 128
NQ = 512
N_GROUP = 8


def place_ends(entries, rng, low, largest):
    longest = entries.shape.index(max(entries.shape))
    spots = []
    for shift in (0, 1):
        where = [jax.random.randint(jax.random.fold_in(rng, axis), (), 0, length) for axis, length in enumerate(entries.shape)]
        where[longest] = (where[longest] + shift) % entries.shape[longest]
        spots.append(tuple(where))
    return entries.at[spots[0]].set(low).at[spots[1]].set(largest)


def block_scale(rng, shape, shards, smallest, top_value):
    loudness, own = 1.0, jax.random.fold_in(rng, 6)
    for dim, shards_of in shards:
        heights = jnp.exp(jax.random.uniform(jax.random.fold_in(own, dim), (shards_of,), jnp.float32, smallest / len(shards), top_value / len(shards)))
        loudness = loudness * jnp.repeat(heights, shape[dim] // shards_of).reshape([-1 if axis == dim else 1 for axis in range(len(shape))])
    return loudness


def cumulative_ranks(amount, slope):
    portions = [(1 << 20) // math.isqrt(standing ** slope) + 1 for standing in range(1, amount + 1)]
    scale = 1 + sum(portions) // (1 << 30)
    return np.cumsum(np.array([max(1, weight // scale) for weight in portions]))


def ranked_ids(own_key, extent, amount, lean):
    table = cumulative_ranks(amount, lean)
    lot = jax.random.randint(jax.random.fold_in(own_key, 1), extent, 0, int(table[amount - 1]))
    rank = jnp.searchsorted(jnp.asarray(table, jnp.int32), lot, side="right")
    return jax.random.permutation(jax.random.fold_in(own_key, 2), amount)[rank].astype(jnp.int32)


def split_up(amount, total, limit, lean):
    loads = [(1 << 20) // math.isqrt(standing ** lean) + 1 for standing in range(2, amount + 1)]
    rest, counts = total - limit - (amount - 1), [1] * (amount - 1)
    while rest > 0:
        movable = [i for i in range(amount - 1) if counts[i] < limit]
        mass, budget = sum([loads[i] for i in movable]), rest
        for i in movable:
            more = min(limit - counts[i], max(1, budget * loads[i] // mass), rest)
            counts[i] = counts[i] + more
            rest = rest - more
    return np.array([limit] + counts)


def uneven_parts(own_key, amount, total, bound, lean):
    if amount == 2:
        one = jax.random.randint(own_key, (), max(1, total - bound), min(bound, total - 1) + 1)
        return jnp.stack([one, total - one])
    tallies = jnp.asarray(split_up(amount, total, bound, lean), jnp.int32)
    couples = (amount - 1) // 2
    giver, receiver = tallies[1:1 + 2 * couples:2], tallies[2:2 + 2 * couples:2]
    margin = jnp.minimum(giver - 1, bound - receiver)
    shifted = jax.random.randint(jax.random.fold_in(own_key, 1), (couples,), 0, 1 << 20) % (margin + 1)
    tallies = tallies.at[1:1 + 2 * couples:2].set(giver - shifted).at[2:2 + 2 * couples:2].set(receiver + shifted)
    return tallies[jax.random.permutation(jax.random.fold_in(own_key, 2), amount)]


def centred(own_key, extent, deviation, most, split=(), kind=jnp.bfloat16):
    array = deviation * jax.random.normal(own_key, extent, jnp.float32)
    if split:
        array = array * block_scale(own_key, extent, split, -0.22, 0.18)
    return jnp.clip(array, -most, most).astype(kind)


def setup_inputs(seed: int = 0) -> dict:
    seeds = jax.random.split(jax.random.key(seed), 10)
    corpus_tokens = centred(seeds[0], (TOKENS, D), 1.0, 6.0, ((0, 256),))
    norm_gain = jnp.clip(1.0 + 0.18 * jax.random.normal(seeds[1], (D,), jnp.float32), 0.1, 1.9)
    wi_weight = centred(seeds[2], (D, 2 * FF), D ** -0.5, 0.1875, ((0, 32),))
    wo_weight = centred(seeds[3], (FF, D), FF ** -0.5, 0.125, ((0, 32),))
    final_gain = jnp.clip(1.0 + 0.18 * jax.random.normal(seeds[4], (D,), jnp.float32), 0.1, 1.9)
    proj_weight = centred(seeds[5], (D, DIM), D ** -0.5, 0.1875)
    query_vectors = centred(seeds[6], (NQ, QT, DIM), 1.0, 6.0, ((0, 256),))
    doc_lengths = jax.vmap(lambda own: uneven_parts(own, DOCS_G, SHARD, DOC_MOST, 2))(jax.random.split(seeds[7], N_GROUP)).reshape((N_GROUP, DOCS_G)).astype(jnp.int32)
    candidates = place_ends(ranked_ids(seeds[8], (NQ, NCAND), NDOCS, 2), jax.random.fold_in(seeds[8], 3), 0, NDOCS - 1).astype(jnp.int32)
    return {"corpus_tokens": corpus_tokens, "norm_gain": norm_gain, "wi_weight": wi_weight, "wo_weight": wo_weight, "final_gain": final_gain, "proj_weight": proj_weight, "query_vectors": query_vectors, "doc_lengths": doc_lengths, "candidates": candidates}


def layer_norm(values, gain_row):
    values = values.astype(jnp.float32)
    center = lax.optimization_barrier(jnp.mean(values, axis=-1, keepdims=True))
    spread = lax.optimization_barrier(jnp.mean(jnp.square(values - center), axis=-1, keepdims=True))
    return (values - center) * lax.rsqrt(spread + 1e-05) * gain_row.astype(jnp.float32)

def encode(tokens, norm_gain, wi_weight, wo_weight, final_gain, proj_weight):
    normed = layer_norm(tokens, norm_gain).astype(jnp.bfloat16)
    lifted = jnp.dot(normed, wi_weight, preferred_element_type=jnp.float32)
    hidden_width = wo_weight.shape[0]
    hidden = (jax.nn.gelu(lifted[:, :hidden_width], approximate=False) * lifted[:, hidden_width:]).astype(jnp.bfloat16)
    mixed_sum = tokens.astype(jnp.float32) + jnp.dot(hidden, wo_weight, preferred_element_type=jnp.float32)
    normed_out = layer_norm(mixed_sum, final_gain).astype(jnp.bfloat16)
    projected = jnp.dot(normed_out, proj_weight, preferred_element_type=jnp.float32)
    inverse = lax.rsqrt(lax.optimization_barrier(jnp.sum(projected * projected, axis=-1, keepdims=True)) + 1e-06)
    return (projected * inverse).astype(jnp.bfloat16)

def document_of(lengths, total_rows):
    doc_ends = jnp.cumsum(lengths.astype(jnp.int32))
    places = jnp.arange(total_rows, dtype=jnp.int32)
    return lax.optimization_barrier(jnp.sum((places[:, None] >= doc_ends[None, :]).astype(jnp.int32), axis=1))

def group_maxima(query_rows, vectors, owners):
    row_block = math.gcd(vectors.shape[0], 2048)
    count_steps = vectors.shape[0] // row_block
    start_value = jnp.full((DOCS_G, query_rows.shape[0]), -jnp.inf, jnp.bfloat16)

    def advance(running, element):
        vector_part, owner_part = element
        similar = jnp.dot(vector_part, query_rows.T, preferred_element_type=jnp.float32).astype(jnp.bfloat16)
        return (running.at[owner_part].max(similar), None)
    outcome, _ = lax.scan(advance, start_value, (vectors.reshape(count_steps, row_block, vectors.shape[1]), owners.reshape(count_steps, row_block)))
    return outcome

def reference(corpus_tokens, norm_gain, wi_weight, wo_weight, final_gain, proj_weight, query_vectors, doc_lengths, candidates):
    grouped = corpus_tokens.reshape(N_GROUP, SHARD, D)
    vectors = lax.map(lambda group_rows: encode(group_rows, norm_gain, wi_weight, wo_weight, final_gain, proj_weight), grouped)
    query_rows = query_vectors.reshape(NQ * QT, DIM)
    owners = jax.vmap(lambda lengths: document_of(lengths, SHARD))(doc_lengths)
    maxima = lax.map(lambda group_pair: group_maxima(query_rows, group_pair[0], group_pair[1]), (vectors, owners))
    doc_scores = lax.optimization_barrier(jnp.sum(maxima.astype(jnp.float32).reshape(N_GROUP, DOCS_G, NQ, QT), axis=-1)) / QT
    score_table = jnp.transpose(doc_scores, (2, 0, 1)).reshape(NQ, NDOCS)
    scores = jnp.take_along_axis(score_table, candidates.astype(jnp.int32), axis=1)
    return (vectors.reshape(TOKENS, DIM), scores)
```

```python
import jax
import jax.numpy as jnp
from jax import lax
from jax.experimental import pallas as pl
from jax.experimental.pallas import tpu as pltpu
from jax.sharding import PartitionSpec as P

BLOCK = 256


def layer_norm(values, gain_row):
    values = values.astype(jnp.float32)
    center = jnp.mean(values, axis=-1, keepdims=True)
    spread = jnp.mean(jnp.square(values - center), axis=-1, keepdims=True)
    return (values - center) * lax.rsqrt(spread + 1e-05) * gain_row


def segment_maxima(ends_ref, vec_ref, query_rows, doc_count):
    tokens = vec_ref.shape[0]
    blocks = tokens // BLOCK
    width = query_rows.shape[0]
    row_ids = lax.broadcasted_iota(jnp.int32, (BLOCK, width), 0)
    doc_ids = lax.broadcasted_iota(jnp.int32, (doc_count, width), 0)

    def step(_, state):
        place, doc, best = state
        block = jnp.minimum(place // BLOCK, blocks - 1)
        first = pl.multiple_of(block * BLOCK, BLOCK)
        doc_end = ends_ref[doc]
        stop = jnp.minimum(doc_end, first + BLOCK)
        similar = lax.dot_general(
            vec_ref[pl.ds(first, BLOCK), :],
            query_rows,
            (((1,), (1,)), ((), ())),
            preferred_element_type=jnp.float32,
        )
        inside = (row_ids >= place - first) & (row_ids < stop - first)
        top = jnp.max(jnp.where(inside, similar, -jnp.inf), axis=0, keepdims=True)
        best = jnp.where(doc_ids == doc, jnp.maximum(best, top), best)
        doc = jnp.minimum(doc + (stop == doc_end).astype(jnp.int32), doc_count - 1)
        return stop, doc, best

    start = jnp.full((doc_count, width), -jnp.inf, jnp.float32)
    state = (jnp.int32(0), jnp.int32(0), start)
    return lax.fori_loop(0, blocks + doc_count - 1, step, state)[2]


def score_kernel(query_len, ends_ref, vec_ref, query_ref, out_ref):
    doc_count = out_ref.shape[0]
    best = segment_maxima(ends_ref, vec_ref, query_ref[...], doc_count).astype(jnp.bfloat16)
    rows = lax.broadcasted_iota(jnp.int32, (best.shape[1], out_ref.shape[1]), 0)
    cols = lax.broadcasted_iota(jnp.int32, (best.shape[1], out_ref.shape[1]), 1)
    adder = (rows // query_len == cols).astype(jnp.bfloat16)
    out_ref[...] = jnp.dot(best, adder, preferred_element_type=jnp.float32) / query_len


def body(
    corpus_tokens,
    norm_gain,
    wi_weight,
    wo_weight,
    final_gain,
    proj_weight,
    query_vectors,
    doc_lengths,
    candidates,
):
    groups = lax.axis_size("group")
    doc_count = doc_lengths.shape[1]
    per_query, query_len, vector_dim = query_vectors.shape
    near_queries = lax.all_gather(query_vectors, "group", axis=0, tiled=True)
    normed = layer_norm(corpus_tokens, norm_gain).astype(jnp.bfloat16)
    lifted = jnp.dot(
        normed,
        lax.all_gather(wi_weight, "dev", axis=0, tiled=True),
        preferred_element_type=jnp.float32,
    )
    hidden_width = wi_weight.shape[1] // 2
    hidden = (
        jax.nn.gelu(lifted[:, :hidden_width], approximate=False) * lifted[:, hidden_width:]
    ).astype(jnp.bfloat16)
    down_sum = jnp.dot(
        hidden,
        lax.all_gather(wo_weight, "dev", axis=0, tiled=True),
        preferred_element_type=jnp.float32,
    )
    mixed_sum = corpus_tokens.astype(jnp.float32) + down_sum
    normed_out = layer_norm(mixed_sum, final_gain).astype(jnp.bfloat16)
    projected = jnp.dot(normed_out, proj_weight, preferred_element_type=jnp.float32)
    inverse = lax.rsqrt(jnp.sum(projected * projected, axis=-1, keepdims=True) + 1e-06)
    vectors = (projected * inverse).astype(jnp.bfloat16)

    group_vectors = lax.all_gather(vectors, "dev", axis=0, tiled=True)
    doc_ends = jnp.cumsum(doc_lengths[0])
    table = pl.pallas_call(
        lambda *refs: score_kernel(query_len, *refs),
        out_shape=jax.ShapeDtypeStruct((doc_count, 128), jnp.float32),
        in_specs=[
            pl.BlockSpec(memory_space=pltpu.SMEM),
            pl.BlockSpec(memory_space=pltpu.VMEM),
            pl.BlockSpec(memory_space=pltpu.VMEM),
        ],
        out_specs=pl.BlockSpec(memory_space=pltpu.VMEM),
        name="score",
    )(doc_ends, group_vectors, near_queries.reshape(-1, vector_dim))
    totals = table[:, : groups * per_query].reshape(doc_count, groups, per_query)
    outgoing = jnp.transpose(totals, (1, 2, 0))
    incoming = lax.all_to_all(outgoing, "group", split_axis=0, concat_axis=0, tiled=True)
    score_table = jnp.transpose(incoming, (1, 0, 2)).reshape(per_query, groups * doc_count)
    labels = jnp.arange(groups * doc_count, dtype=jnp.int32)
    picked = (candidates[:, :, None] == labels[None, None, :]).astype(jnp.float32)
    scores = jnp.sum(picked * score_table[:, None, :], axis=-1)
    return (vectors, scores)


def solution(mesh):
    placed = (
        P(("group", "dev"), None),
        P(),
        P("dev", None),
        P("dev", None),
        P(),
        P(),
        P(("group", "dev"), None, None),
        P("group", None),
        P(("group", "dev"), None),
    )
    return jax.shard_map(
        body,
        mesh=mesh,
        in_specs=placed,
        out_specs=(P(("group", "dev"), None), P(("group", "dev"), None)),
        check_vma=False,
    )
```

```python
import jax
import jax.numpy as jnp
from jax import lax
from jax.experimental import pallas as pl
from jax.experimental.pallas import tpu as pltpu
from jax.sharding import PartitionSpec as P

BLOCK = 256


def layer_norm(values, gain_row):
    values = values.astype(jnp.float32)
    center = jnp.mean(values, axis=-1, keepdims=True)
    spread = jnp.mean(jnp.square(values - center), axis=-1, keepdims=True)
    return (values - center) * lax.rsqrt(spread + 1e-05) * gain_row


def segment_maxima(ends_ref, vec_ref, query_rows, doc_count):
    tokens = vec_ref.shape[0]
    blocks = tokens // BLOCK
    width = query_rows.shape[0]
    row_ids = lax.broadcasted_iota(jnp.int32, (BLOCK, width), 0)
    doc_ids = lax.broadcasted_iota(jnp.int32, (doc_count, width), 0)

    def step(_, state):
        place, doc, best = state
        block = jnp.minimum(place // BLOCK, blocks - 1)
        first = pl.multiple_of(block * BLOCK, BLOCK)
        doc_end = ends_ref[doc]
        stop = jnp.minimum(doc_end, first + BLOCK)
        similar = lax.dot_general(
            vec_ref[pl.ds(first, BLOCK), :],
            query_rows,
            (((1,), (1,)), ((), ())),
            preferred_element_type=jnp.float32,
        )
        inside = (row_ids >= place - first) & (row_ids < stop - first)
        top = jnp.max(jnp.where(inside, similar, -jnp.inf), axis=0, keepdims=True)
        best = jnp.where(doc_ids == doc, jnp.maximum(best, top), best)
        doc = jnp.minimum(doc + (stop == doc_end).astype(jnp.int32), doc_count - 1)
        return stop, doc, best

    start = jnp.full((doc_count, width), -jnp.inf, jnp.float32)
    state = (jnp.int32(0), jnp.int32(0), start)
    return lax.fori_loop(0, blocks + doc_count - 1, step, state)[2]


def score_kernel(query_len, ends_ref, vec_ref, query_ref, out_ref):
    doc_count = out_ref.shape[0]
    best = segment_maxima(ends_ref, vec_ref, query_ref[...], doc_count).astype(jnp.bfloat16)
    rows = lax.broadcasted_iota(jnp.int32, (best.shape[1], out_ref.shape[1]), 0)
    cols = lax.broadcasted_iota(jnp.int32, (best.shape[1], out_ref.shape[1]), 1)
    adder = (rows // query_len == cols).astype(jnp.bfloat16)
    out_ref[...] = jnp.dot(best, adder, preferred_element_type=jnp.float32) / query_len


MESH = pl.DeviceIdType.MESH
SIDE = 4
OFFSETS = (0, -1, 1, 2)


def place():
    dev = lax.axis_index("dev")
    core = dev % 2
    chip = dev // 2
    x, y = chip // SIDE, chip % SIDE

    def at(dx, dy):
        return (((x + dx + SIDE) % SIDE) * SIDE + (y + dy + SIDE) % SIDE) * 2 + core

    return dev, dev + 1 - 2 * core, 1 - 2 * core, at


def greet(targets):
    barrier = pltpu.get_barrier_semaphore()
    for target in targets:
        pl.semaphore_signal(barrier, inc=1, device_id=target, device_id_type=MESH)
    pl.semaphore_wait(barrier, len(targets))


def remote(src, dst, send_sem, recv_sem, target):
    return pltpu.make_async_remote_copy(
        src_ref=src,
        dst_ref=dst,
        send_sem=send_sem,
        recv_sem=recv_sem,
        device_id=target,
        device_id_type=MESH,
    )


def weights_kernel(
    groups, wi, wo, query, wi_out, wo_out, query_out,
    ring_send, ring_recv, pair_send, pair_recv, query_send, query_recv, own_sem,
):
    dev, partner, flip, at = place()
    group = lax.axis_index("group")
    depth, width = wi.shape
    half_depth = depth // 2
    cut = (width // 256) * 128 + 128
    model = wo.shape[1]
    rows = query.shape[0]
    sent = []

    def loc(p, first, second):
        return at(first, second) if p == 0 else at(second, first)

    def views(origin, p, half):
        wi_cols = {None: (0, width), 0: (0, cut), 1: (cut, width - cut)}[half]
        wo_cols = (p * model // 2 + (model // 4 if half == 1 else 0), model // (2 if half is None else 4))
        if origin is None:
            return (
                wi.at[pl.ds(p * half_depth, half_depth), pl.ds(*wi_cols)],
                wo.at[:, pl.ds(*wo_cols)],
            )
        first = pl.multiple_of(origin * depth + p * half_depth, half_depth)
        return (
            wi_out.at[pl.ds(first, half_depth), pl.ds(*wi_cols)],
            wo_out.at[origin, :, pl.ds(*wo_cols)],
        )

    def copies(source, origin, p, half, sems_send, sems_recv, index, target):
        pairs = zip(views(source, p, half), views(origin, p, half))
        return [
            remote(src, dst, sems_send.at[index, i], sems_recv.at[index, i], {"dev": target})
            for i, (src, dst) in enumerate(pairs)
        ]

    def ring_index(p, slot, kind):
        return (p * 5 + slot) * 4 + kind

    def start(*args):
        for copy in copies(*args):
            copy.start()
            sent.append(copy)

    def ring_start(p, slot, source, origin):
        for kind, step in ((0, 1), (1, -1)):
            target = loc(p, step, 0) if slot == 0 else loc(p, 0, step)
            start(source, origin, p, None, ring_send, ring_recv, ring_index(p, slot, kind), target)

    def ring_pass(p, slot, kind, origin):
        step = 1 if kind == 0 else -1
        target = loc(p, step, 0) if slot == 0 else loc(p, 0, step)
        start(origin, origin, p, kind, ring_send, ring_recv, ring_index(p, slot, kind + 2), target)

    def ring_wait(p, slot, kind, origin):
        half = kind - 2 if kind >= 2 else None
        for copy in copies(origin, origin, p, half, ring_send, ring_recv, ring_index(p, slot, kind), partner):
            copy.wait_recv()

    def pair_index(p, first, second):
        return (p * 4 + OFFSETS.index(first)) * 4 + OFFSETS.index(second)

    def pair_start(p, first, second, source, origin):
        start(source, origin, p, None, pair_send, pair_recv, pair_index(p, first, second), partner)

    others = [(group + k) % groups for k in range(1, groups)]
    greet(
        [{"dev": at(*d)} for d in ((1, 0), (-1, 0), (0, 1), (0, -1))]
        + [{"dev": partner}]
        + [{"group": other} for other in others]
    )
    for p in (0, 1):
        ring_start(p, 0, None, dev)
    for p in (0, 1):
        ring_start(p, 1, None, dev)
        pair_start(p, 0, 0, None, dev)
    own_rows = pl.ds(pl.multiple_of(group * rows, rows), rows)
    for k, other in enumerate(others):
        copy = remote(query, query_out.at[own_rows], query_send.at[k], query_recv.at[k], {"group": other})
        copy.start()
        sent.append(copy)
    kept = [
        pltpu.make_async_copy(wi, wi_out.at[pl.ds(pl.multiple_of(dev * depth, depth), depth)], own_sem.at[0]),
        pltpu.make_async_copy(wo, wo_out.at[dev], own_sem.at[1]),
        pltpu.make_async_copy(query, query_out.at[own_rows], own_sem.at[2]),
    ]
    for copy in kept:
        copy.start()

    for slot, first, kind in ((2, -1, 0), (3, 1, 1)):
        for p in (0, 1):
            origin = loc(p, first, 0)
            ring_wait(p, 0, kind, origin)
            ring_pass(p, 0, kind, origin)
            ring_start(p, slot, origin, origin)
            pair_start(p, first, 0, origin, origin)
    for p in (0, 1):
        origin = loc(p, 2, 0)
        ring_wait(p, 0, 2, origin)
        ring_wait(p, 0, 3, origin)
        ring_start(p, 4, origin, origin)
        pair_start(p, 2, 0, origin, origin)
    for slot, first in ((1, 0), (2, -1), (3, 1), (4, 2)):
        for second, kind in ((-1, 0), (1, 1)):
            for p in (0, 1):
                origin = loc(p, first, second)
                ring_wait(p, slot, kind, origin)
                ring_pass(p, slot, kind, origin)
                pair_start(p, first, second, origin, origin)
    for slot, first in ((1, 0), (2, -1), (3, 1), (4, 2)):
        for p in (0, 1):
            origin = loc(p, first, 2)
            ring_wait(p, slot, 2, origin)
            ring_wait(p, slot, 3, origin)
            pair_start(p, first, 2, origin, origin)

    for k in range(groups - 1):
        source = (group + groups - 1 - k) % groups
        landing = query_out.at[pl.ds(pl.multiple_of(source * rows, rows), rows)]
        remote(query, landing, query_send.at[k], query_recv.at[k], {"dev": partner}).wait_recv()
    for first in OFFSETS:
        for second in OFFSETS:
            for p in (0, 1):
                origin = loc(p, first, second) + flip
                index = pair_index(p, first, second)
                for copy in copies(origin, origin, p, None, pair_send, pair_recv, index, partner):
                    copy.wait_recv()
    for copy in sent:
        copy.wait_send()
    for copy in kept:
        copy.wait()


def gather_weights(wi_weight, wo_weight, query_rows, groups, devs):
    depth, width = wi_weight.shape
    kept_rows, model = wo_weight.shape
    rows, vector_dim = query_rows.shape
    return pl.pallas_call(
        lambda *refs: weights_kernel(groups, *refs),
        out_shape=(
            jax.ShapeDtypeStruct((devs * depth, width), wi_weight.dtype),
            jax.ShapeDtypeStruct((devs, kept_rows, model), wo_weight.dtype),
            jax.ShapeDtypeStruct((groups * rows, vector_dim), query_rows.dtype),
        ),
        in_specs=[pl.BlockSpec(memory_space=pltpu.VMEM)] * 3,
        out_specs=[pl.BlockSpec(memory_space=pl.ANY)] * 3,
        scratch_shapes=[
            pltpu.SemaphoreType.DMA((40, 2)),
            pltpu.SemaphoreType.DMA((40, 2)),
            pltpu.SemaphoreType.DMA((32, 2)),
            pltpu.SemaphoreType.DMA((32, 2)),
            pltpu.SemaphoreType.DMA((groups - 1,)),
            pltpu.SemaphoreType.DMA((groups - 1,)),
            pltpu.SemaphoreType.DMA((3,)),
        ],
        compiler_params=pltpu.CompilerParams(collective_id=0, has_side_effects=True),
        name="weights",
    )(wi_weight, wo_weight, query_rows)


def vectors_kernel(vec, out, send_sem, recv_sem, pair_send, pair_recv, own_sem):
    dev, partner, flip, at = place()
    rows = vec.shape[0]

    def block(origin):
        return out.at[pl.ds(pl.multiple_of(origin * rows, rows), rows)]

    steps = [(dx, dy) for dx in OFFSETS for dy in OFFSETS if (dx, dy) != (0, 0)]
    steps.sort(key=lambda d: -abs(d[0]) - abs(d[1]))
    greet([{"dev": at(dx, dy)} for dx, dy in steps] + [{"dev": partner}])
    sent = []
    for k, (dx, dy) in enumerate(steps):
        sent.append(remote(vec, block(dev), send_sem.at[k], recv_sem.at[k], {"dev": at(dx, dy)}))
        sent[-1].start()
    sent.append(remote(vec, block(dev), pair_send.at[15], pair_recv.at[15], {"dev": partner}))
    sent[-1].start()
    kept = pltpu.make_async_copy(vec, block(dev), own_sem)
    kept.start()
    for k, (dx, dy) in reversed(list(enumerate(steps))):
        origin = at(-dx, -dy)
        remote(vec, block(origin), send_sem.at[k], recv_sem.at[k], {"dev": partner}).wait_recv()
        sent.append(remote(block(origin), block(origin), pair_send.at[k], pair_recv.at[k], {"dev": partner}))
        sent[-1].start()
    for k, (dx, dy) in enumerate(steps + [(0, 0)]):
        origin = at(-dx, -dy) + flip
        remote(vec, block(origin), pair_send.at[k], pair_recv.at[k], {"dev": partner}).wait_recv()
    for copy in sent:
        copy.wait_send()
    kept.wait()


def gather_vectors(vectors, devs):
    rows, vector_dim = vectors.shape
    return pl.pallas_call(
        vectors_kernel,
        out_shape=jax.ShapeDtypeStruct((devs * rows, vector_dim), vectors.dtype),
        in_specs=[pl.BlockSpec(memory_space=pltpu.VMEM)],
        out_specs=pl.BlockSpec(memory_space=pltpu.VMEM),
        scratch_shapes=[
            pltpu.SemaphoreType.DMA((15,)),
            pltpu.SemaphoreType.DMA((15,)),
            pltpu.SemaphoreType.DMA((16,)),
            pltpu.SemaphoreType.DMA((16,)),
            pltpu.SemaphoreType.DMA,
        ],
        compiler_params=pltpu.CompilerParams(collective_id=1, has_side_effects=True),
        name="vectors",
    )(vectors)


def pick_kernel(groups, table, wanted, out, tables, send_sem, recv_sem, own_sem):
    group = lax.axis_index("group")
    others = [(group + k) % groups for k in range(1, groups)]
    greet([{"group": other} for other in others])
    sent = []
    for k, other in enumerate(others):
        sent.append(remote(table, tables.at[group], send_sem.at[k], recv_sem.at[k], {"group": other}))
        sent[-1].start()
    kept = pltpu.make_async_copy(table, tables.at[group], own_sem)
    kept.start()
    per_query, listed = wanted.shape
    docs = table.shape[0]
    for k in range(groups - 1):
        source = (group + groups - 1 - k) % groups
        remote(table, tables.at[source], send_sem.at[k], recv_sem.at[k], {"group": other}).wait_recv()
    kept.wait()
    for copy in sent:
        copy.wait_send()
    lanes = lax.broadcasted_iota(jnp.int32, (docs, table.shape[1]), 1)
    labels = lax.broadcasted_iota(jnp.int32, (docs, listed), 0)
    for q in range(per_query):
        row = wanted[pl.ds(q, 1), :]
        total = jnp.zeros((1, listed), jnp.float32)
        for g in range(groups):
            mine = jnp.where(lanes == group * per_query + q, tables[g], 0.0)
            column = jnp.sum(mine, axis=1, keepdims=True)
            hit = jnp.where(labels + g * docs == row, column, 0.0)
            total = total + jnp.sum(hit, axis=0, keepdims=True)
        out[pl.ds(q, 1), :] = total


def pick_scores(table, candidates, groups):
    return pl.pallas_call(
        lambda *refs: pick_kernel(groups, *refs),
        out_shape=jax.ShapeDtypeStruct(candidates.shape, jnp.float32),
        in_specs=[pl.BlockSpec(memory_space=pltpu.VMEM)] * 2,
        out_specs=pl.BlockSpec(memory_space=pltpu.VMEM),
        scratch_shapes=[
            pltpu.VMEM((groups,) + table.shape, jnp.float32),
            pltpu.SemaphoreType.DMA((groups - 1,)),
            pltpu.SemaphoreType.DMA((groups - 1,)),
            pltpu.SemaphoreType.DMA,
        ],
        compiler_params=pltpu.CompilerParams(collective_id=2, has_side_effects=True),
        name="pick",
    )(table, candidates)


def body(
    corpus_tokens,
    norm_gain,
    wi_weight,
    wo_weight,
    final_gain,
    proj_weight,
    query_vectors,
    doc_lengths,
    candidates,
):
    groups = lax.axis_size("group")
    doc_count = doc_lengths.shape[1]
    per_query, query_len, vector_dim = query_vectors.shape
    devs = lax.axis_size("dev")
    wi_full, wo_blocks, near_queries = gather_weights(
        wi_weight, wo_weight, query_vectors.reshape(-1, vector_dim), groups, devs
    )
    normed = layer_norm(corpus_tokens, norm_gain).astype(jnp.bfloat16)
    lifted = jnp.dot(
        normed,
        wi_full,
        preferred_element_type=jnp.float32,
    )
    hidden_width = wi_weight.shape[1] // 2
    hidden = (
        jax.nn.gelu(lifted[:, :hidden_width], approximate=False) * lifted[:, hidden_width:]
    ).astype(jnp.bfloat16)
    down_sum = jnp.dot(
        hidden,
        wo_blocks.reshape(hidden_width, -1),
        preferred_element_type=jnp.float32,
    )
    mixed_sum = corpus_tokens.astype(jnp.float32) + down_sum
    normed_out = layer_norm(mixed_sum, final_gain).astype(jnp.bfloat16)
    projected = jnp.dot(normed_out, proj_weight, preferred_element_type=jnp.float32)
    inverse = lax.rsqrt(jnp.sum(projected * projected, axis=-1, keepdims=True) + 1e-06)
    vectors = (projected * inverse).astype(jnp.bfloat16)

    group_vectors = gather_vectors(vectors, devs)
    doc_ends = jnp.cumsum(doc_lengths[0])
    table = pl.pallas_call(
        lambda *refs: score_kernel(query_len, *refs),
        out_shape=jax.ShapeDtypeStruct((doc_count, 128), jnp.float32),
        in_specs=[
            pl.BlockSpec(memory_space=pltpu.SMEM),
            pl.BlockSpec(memory_space=pltpu.VMEM),
            pl.BlockSpec(memory_space=pltpu.VMEM),
        ],
        out_specs=pl.BlockSpec(memory_space=pltpu.VMEM),
        name="score",
    )(doc_ends, group_vectors, near_queries)
    scores = pick_scores(table, candidates, groups)
    return (vectors, scores)


def solution(mesh):
    placed = (
        P(("group", "dev"), None),
        P(),
        P("dev", None),
        P("dev", None),
        P(),
        P(),
        P(("group", "dev"), None, None),
        P("group", None),
        P(("group", "dev"), None),
    )
    return jax.shard_map(
        body,
        mesh=mesh,
        in_specs=placed,
        out_specs=(P(("group", "dev"), None), P(("group", "dev"), None)),
        check_vma=False,
    )
```

```python
import jax
import jax.numpy as jnp
from jax import lax
from jax.experimental import pallas as pl
from jax.experimental.pallas import tpu as pltpu
from jax.sharding import PartitionSpec as P

BLOCK = 256


def layer_norm(values, gain_row):
    values = values.astype(jnp.float32)
    center = jnp.mean(values, axis=-1, keepdims=True)
    spread = jnp.mean(jnp.square(values - center), axis=-1, keepdims=True)
    return (values - center) * lax.rsqrt(spread + 1e-05) * gain_row


def segment_maxima(ends_ref, vec_ref, query_rows, doc_count):
    tokens = vec_ref.shape[0]
    blocks = tokens // BLOCK
    width = query_rows.shape[0]
    row_ids = lax.broadcasted_iota(jnp.int32, (BLOCK, width), 0)
    doc_ids = lax.broadcasted_iota(jnp.int32, (doc_count, width), 0)

    def step(_, state):
        place, doc, best = state
        block = jnp.minimum(place // BLOCK, blocks - 1)
        first = pl.multiple_of(block * BLOCK, BLOCK)
        doc_end = ends_ref[doc]
        stop = jnp.minimum(doc_end, first + BLOCK)
        similar = lax.dot_general(
            vec_ref[pl.ds(first, BLOCK), :],
            query_rows,
            (((1,), (1,)), ((), ())),
            preferred_element_type=jnp.float32,
        )
        inside = (row_ids >= place - first) & (row_ids < stop - first)
        top = jnp.max(jnp.where(inside, similar, -jnp.inf), axis=0, keepdims=True)
        best = jnp.where(doc_ids == doc, jnp.maximum(best, top), best)
        doc = jnp.minimum(doc + (stop == doc_end).astype(jnp.int32), doc_count - 1)
        return stop, doc, best

    start = jnp.full((doc_count, width), -jnp.inf, jnp.float32)
    state = (jnp.int32(0), jnp.int32(0), start)
    return lax.fori_loop(0, blocks + doc_count - 1, step, state)[2]


def score_kernel(query_len, ends_ref, vec_ref, query_ref, out_ref):
    doc_count = out_ref.shape[0]
    best = segment_maxima(ends_ref, vec_ref, query_ref[...], doc_count).astype(jnp.bfloat16)
    rows = lax.broadcasted_iota(jnp.int32, (best.shape[1], out_ref.shape[1]), 0)
    cols = lax.broadcasted_iota(jnp.int32, (best.shape[1], out_ref.shape[1]), 1)
    adder = (rows // query_len == cols).astype(jnp.bfloat16)
    out_ref[...] = jnp.dot(best, adder, preferred_element_type=jnp.float32) / query_len


MESH = pl.DeviceIdType.MESH
SIDE = 4
OFFSETS = (0, -1, 1, 2)
TILE = 512


def place():
    dev = lax.axis_index("dev")
    core = dev % 2
    chip = dev // 2
    x, y = chip // SIDE, chip % SIDE

    def at(dx, dy):
        return (((x + dx + SIDE) % SIDE) * SIDE + (y + dy + SIDE) % SIDE) * 2 + core

    return dev, dev + 1 - 2 * core, 1 - 2 * core, at


def greet(targets):
    barrier = pltpu.get_barrier_semaphore()
    for target in targets:
        pl.semaphore_signal(barrier, inc=1, device_id=target, device_id_type=MESH)
    pl.semaphore_wait(barrier, len(targets))


def remote(src, dst, send_sem, recv_sem, target):
    return pltpu.make_async_remote_copy(
        src_ref=src,
        dst_ref=dst,
        send_sem=send_sem,
        recv_sem=recv_sem,
        device_id=target,
        device_id_type=MESH,
    )


def weights_kernel(
    groups, wi, wo, query, tokens, norm_gain, final_gain, proj, query_out, vec_out,
    wi_out, wo_out, normed, lifted, hidden, mixed,
    ring_send, ring_recv, pair_send, pair_recv, query_send, query_recv, own_sem,
):
    dev, partner, flip, at = place()
    group = lax.axis_index("group")
    depth, width = wi.shape
    half_depth = depth // 2
    cut = (width // 256) * 128 + 128
    model = wo.shape[1]
    rows = query.shape[0]
    sent = []

    def loc(p, first, second):
        return at(first, second) if p == 0 else at(second, first)

    def views(origin, p, half):
        wi_cols = {None: (0, width), 0: (0, cut), 1: (cut, width - cut)}[half]
        wo_cols = (p * model // 2 + (model // 4 if half == 1 else 0), model // (2 if half is None else 4))
        if origin is None:
            return (
                wi.at[pl.ds(p * half_depth, half_depth), pl.ds(*wi_cols)],
                wo.at[:, pl.ds(*wo_cols)],
            )
        first = pl.multiple_of(origin * depth + p * half_depth, half_depth)
        return (
            wi_out.at[pl.ds(first, half_depth), pl.ds(*wi_cols)],
            wo_out.at[origin, :, pl.ds(*wo_cols)],
        )

    def copies(source, origin, p, half, sems_send, sems_recv, index, target):
        pairs = zip(views(source, p, half), views(origin, p, half))
        return [
            remote(src, dst, sems_send.at[index, i], sems_recv.at[index, i], {"dev": target})
            for i, (src, dst) in enumerate(pairs)
        ]

    def ring_index(p, slot, kind):
        return (p * 5 + slot) * 4 + kind

    def start(*args):
        for copy in copies(*args):
            copy.start()
            sent.append(copy)

    def ring_start(p, slot, source, origin):
        for kind, step in ((0, 1), (1, -1)):
            target = loc(p, step, 0) if slot == 0 else loc(p, 0, step)
            start(source, origin, p, None, ring_send, ring_recv, ring_index(p, slot, kind), target)

    def ring_pass(p, slot, kind, origin):
        step = 1 if kind == 0 else -1
        target = loc(p, step, 0) if slot == 0 else loc(p, 0, step)
        start(origin, origin, p, kind, ring_send, ring_recv, ring_index(p, slot, kind + 2), target)

    def ring_wait(p, slot, kind, origin):
        half = kind - 2 if kind >= 2 else None
        for copy in copies(origin, origin, p, half, ring_send, ring_recv, ring_index(p, slot, kind), partner):
            copy.wait_recv()

    def pair_index(p, first, second):
        return (p * 4 + OFFSETS.index(first)) * 4 + OFFSETS.index(second)

    def pair_start(p, first, second, source, origin):
        start(source, origin, p, None, pair_send, pair_recv, pair_index(p, first, second), partner)

    others = [(group + k) % groups for k in range(1, groups)]
    greet(
        [{"dev": at(*d)} for d in ((1, 0), (-1, 0), (0, 1), (0, -1))]
        + [{"dev": partner}]
        + [{"group": other} for other in others]
    )
    for p in (0, 1):
        ring_start(p, 0, None, dev)
    for p in (0, 1):
        ring_start(p, 1, None, dev)
        pair_start(p, 0, 0, None, dev)
    own_rows = pl.ds(pl.multiple_of(group * rows, rows), rows)
    for k, other in enumerate(others):
        copy = remote(query, query_out.at[own_rows], query_send.at[k], query_recv.at[k], {"group": other})
        copy.start()
        sent.append(copy)
    kept = [
        pltpu.make_async_copy(wi, wi_out.at[pl.ds(pl.multiple_of(dev * depth, depth), depth)], own_sem.at[0]),
        pltpu.make_async_copy(wo, wo_out.at[dev], own_sem.at[1]),
        pltpu.make_async_copy(query, query_out.at[own_rows], own_sem.at[2]),
    ]
    for copy in kept:
        copy.start()
    normed[...] = layer_norm(tokens[...], norm_gain[...]).astype(jnp.bfloat16)

    for slot, first, kind in ((2, -1, 0), (3, 1, 1)):
        for p in (0, 1):
            origin = loc(p, first, 0)
            ring_wait(p, 0, kind, origin)
            ring_pass(p, 0, kind, origin)
            ring_start(p, slot, origin, origin)
            pair_start(p, first, 0, origin, origin)
    for p in (0, 1):
        origin = loc(p, 2, 0)
        ring_wait(p, 0, 2, origin)
        ring_wait(p, 0, 3, origin)
        ring_start(p, 4, origin, origin)
        pair_start(p, 2, 0, origin, origin)
    for slot, first in ((1, 0), (2, -1), (3, 1), (4, 2)):
        for second, kind in ((-1, 0), (1, 1)):
            for p in (0, 1):
                origin = loc(p, first, second)
                ring_wait(p, slot, kind, origin)
                ring_pass(p, slot, kind, origin)
                pair_start(p, first, second, origin, origin)
    for slot, first in ((1, 0), (2, -1), (3, 1), (4, 2)):
        for p in (0, 1):
            origin = loc(p, first, 2)
            ring_wait(p, slot, 2, origin)
            ring_wait(p, slot, 3, origin)
            pair_start(p, first, 2, origin, origin)

    for k in range(groups - 1):
        source = (group + groups - 1 - k) % groups
        landing = query_out.at[pl.ds(pl.multiple_of(source * rows, rows), rows)]
        remote(query, landing, query_send.at[k], query_recv.at[k], {"dev": partner}).wait_recv()
    for first in OFFSETS:
        for second in OFFSETS:
            for p in (0, 1):
                origin = loc(p, first, second) + flip
                index = pair_index(p, first, second)
                for copy in copies(origin, origin, p, None, pair_send, pair_recv, index, partner):
                    copy.wait_recv()
    for copy in kept:
        copy.wait()

    @pl.loop(0, width // TILE)
    def _(j):
        cols = pl.ds(pl.multiple_of(j * TILE, TILE), TILE)
        lifted[:, cols] = jnp.dot(normed[...], wi_out[:, cols], preferred_element_type=jnp.float32)

    if width % TILE:
        cols = pl.ds(width - width % TILE, width % TILE)
        lifted[:, cols] = jnp.dot(normed[...], wi_out[:, cols], preferred_element_type=jnp.float32)

    @pl.loop(0, hidden.shape[0] // 16)
    def _(i):
        strip = pl.ds(pl.multiple_of(i * 16, 16), 16)
        both = lifted[strip, :]
        gated = both[:, : width // 2]
        gelu = 0.5 * gated * (1.0 + lax.erf(gated * 0.5**0.5))
        hidden[strip, :] = (gelu * both[:, width // 2 :]).astype(jnp.bfloat16)

    mixed[...] = tokens[...].astype(jnp.float32)
    kept_rows = wo.shape[0]
    for k in range(0, wo_out.shape[0], 4):
        part = None
        for i in range(k, k + 4):
            term = jnp.dot(
                hidden[:, i * kept_rows : (i + 1) * kept_rows],
                wo_out[i],
                preferred_element_type=jnp.float32,
            )
            part = term if part is None else part + term
        mixed[...] += part
    normed_out = layer_norm(mixed[...], final_gain[...]).astype(jnp.bfloat16)
    projected = jnp.dot(normed_out, proj[...], preferred_element_type=jnp.float32)
    inverse = lax.rsqrt(jnp.sum(projected * projected, axis=-1, keepdims=True) + 1e-06)
    vec_out[...] = (projected * inverse).astype(jnp.bfloat16)
    for copy in sent:
        copy.wait_send()


def encode(wi_weight, wo_weight, query_rows, tokens, norm_gain, final_gain, proj, groups, devs):
    depth, width = wi_weight.shape
    kept_rows, model = wo_weight.shape
    rows, vector_dim = query_rows.shape
    return pl.pallas_call(
        lambda *refs: weights_kernel(groups, *refs),
        out_shape=(
            jax.ShapeDtypeStruct((groups * rows, vector_dim), query_rows.dtype),
            jax.ShapeDtypeStruct((tokens.shape[0], vector_dim), jnp.bfloat16),
        ),
        in_specs=[pl.BlockSpec(memory_space=pltpu.VMEM)] * 7,
        out_specs=[pl.BlockSpec(memory_space=pltpu.VMEM)] * 2,
        scratch_shapes=[
            pltpu.VMEM((devs * depth, width), wi_weight.dtype),
            pltpu.VMEM((devs, kept_rows, model), wo_weight.dtype),
            pltpu.VMEM(tokens.shape, jnp.bfloat16),
            pltpu.VMEM((tokens.shape[0], width), jnp.float32),
            pltpu.VMEM((tokens.shape[0], width // 2), jnp.bfloat16),
            pltpu.VMEM(tokens.shape, jnp.float32),
            pltpu.SemaphoreType.DMA((40, 2)),
            pltpu.SemaphoreType.DMA((40, 2)),
            pltpu.SemaphoreType.DMA((32, 2)),
            pltpu.SemaphoreType.DMA((32, 2)),
            pltpu.SemaphoreType.DMA((groups - 1,)),
            pltpu.SemaphoreType.DMA((groups - 1,)),
            pltpu.SemaphoreType.DMA((3,)),
        ],
        compiler_params=pltpu.CompilerParams(collective_id=0, has_side_effects=True),
        name="encode",
    )(wi_weight, wo_weight, query_rows, tokens, norm_gain, final_gain, proj)


def vectors_kernel(vec, out, send_sem, recv_sem, pair_send, pair_recv, own_sem):
    dev, partner, flip, at = place()
    rows = vec.shape[0]

    def block(origin):
        return out.at[pl.ds(pl.multiple_of(origin * rows, rows), rows)]

    steps = [(dx, dy) for dx in OFFSETS for dy in OFFSETS if (dx, dy) != (0, 0)]
    steps.sort(key=lambda d: -abs(d[0]) - abs(d[1]))
    greet([{"dev": at(dx, dy)} for dx, dy in steps] + [{"dev": partner}])
    sent = []
    for k, (dx, dy) in enumerate(steps):
        sent.append(remote(vec, block(dev), send_sem.at[k], recv_sem.at[k], {"dev": at(dx, dy)}))
        sent[-1].start()
    sent.append(remote(vec, block(dev), pair_send.at[15], pair_recv.at[15], {"dev": partner}))
    sent[-1].start()
    kept = pltpu.make_async_copy(vec, block(dev), own_sem)
    kept.start()
    for k, (dx, dy) in reversed(list(enumerate(steps))):
        origin = at(-dx, -dy)
        remote(vec, block(origin), send_sem.at[k], recv_sem.at[k], {"dev": partner}).wait_recv()
        sent.append(remote(block(origin), block(origin), pair_send.at[k], pair_recv.at[k], {"dev": partner}))
        sent[-1].start()
    for k, (dx, dy) in enumerate(steps + [(0, 0)]):
        origin = at(-dx, -dy) + flip
        remote(vec, block(origin), pair_send.at[k], pair_recv.at[k], {"dev": partner}).wait_recv()
    for copy in sent:
        copy.wait_send()
    kept.wait()


def gather_vectors(vectors, devs):
    rows, vector_dim = vectors.shape
    return pl.pallas_call(
        vectors_kernel,
        out_shape=jax.ShapeDtypeStruct((devs * rows, vector_dim), vectors.dtype),
        in_specs=[pl.BlockSpec(memory_space=pltpu.VMEM)],
        out_specs=pl.BlockSpec(memory_space=pltpu.VMEM),
        scratch_shapes=[
            pltpu.SemaphoreType.DMA((15,)),
            pltpu.SemaphoreType.DMA((15,)),
            pltpu.SemaphoreType.DMA((16,)),
            pltpu.SemaphoreType.DMA((16,)),
            pltpu.SemaphoreType.DMA,
        ],
        compiler_params=pltpu.CompilerParams(collective_id=1, has_side_effects=True),
        name="vectors",
    )(vectors)


def pick_kernel(groups, table, wanted, out, tables, send_sem, recv_sem, own_sem):
    group = lax.axis_index("group")
    others = [(group + k) % groups for k in range(1, groups)]
    greet([{"group": other} for other in others])
    sent = []
    for k, other in enumerate(others):
        sent.append(remote(table, tables.at[group], send_sem.at[k], recv_sem.at[k], {"group": other}))
        sent[-1].start()
    kept = pltpu.make_async_copy(table, tables.at[group], own_sem)
    kept.start()
    per_query, listed = wanted.shape
    docs = table.shape[0]
    for k in range(groups - 1):
        source = (group + groups - 1 - k) % groups
        remote(table, tables.at[source], send_sem.at[k], recv_sem.at[k], {"group": other}).wait_recv()
    kept.wait()
    for copy in sent:
        copy.wait_send()
    lanes = lax.broadcasted_iota(jnp.int32, (docs, table.shape[1]), 1)
    labels = lax.broadcasted_iota(jnp.int32, (docs, listed), 0)
    for q in range(per_query):
        row = wanted[pl.ds(q, 1), :]
        total = jnp.zeros((1, listed), jnp.float32)
        for g in range(groups):
            mine = jnp.where(lanes == group * per_query + q, tables[g], 0.0)
            column = jnp.sum(mine, axis=1, keepdims=True)
            hit = jnp.where(labels + g * docs == row, column, 0.0)
            total = total + jnp.sum(hit, axis=0, keepdims=True)
        out[pl.ds(q, 1), :] = total


def pick_scores(table, candidates, groups):
    return pl.pallas_call(
        lambda *refs: pick_kernel(groups, *refs),
        out_shape=jax.ShapeDtypeStruct(candidates.shape, jnp.float32),
        in_specs=[pl.BlockSpec(memory_space=pltpu.VMEM)] * 2,
        out_specs=pl.BlockSpec(memory_space=pltpu.VMEM),
        scratch_shapes=[
            pltpu.VMEM((groups,) + table.shape, jnp.float32),
            pltpu.SemaphoreType.DMA((groups - 1,)),
            pltpu.SemaphoreType.DMA((groups - 1,)),
            pltpu.SemaphoreType.DMA,
        ],
        compiler_params=pltpu.CompilerParams(collective_id=2, has_side_effects=True),
        name="pick",
    )(table, candidates)


def body(
    corpus_tokens,
    norm_gain,
    wi_weight,
    wo_weight,
    final_gain,
    proj_weight,
    query_vectors,
    doc_lengths,
    candidates,
):
    groups = lax.axis_size("group")
    doc_count = doc_lengths.shape[1]
    per_query, query_len, vector_dim = query_vectors.shape
    devs = lax.axis_size("dev")
    near_queries, vectors = encode(
        wi_weight,
        wo_weight,
        query_vectors.reshape(-1, vector_dim),
        corpus_tokens,
        norm_gain.reshape(1, -1),
        final_gain.reshape(1, -1),
        proj_weight,
        groups,
        devs,
    )
    group_vectors = gather_vectors(vectors, devs)
    doc_ends = jnp.cumsum(doc_lengths[0])
    table = pl.pallas_call(
        lambda *refs: score_kernel(query_len, *refs),
        out_shape=jax.ShapeDtypeStruct((doc_count, 128), jnp.float32),
        in_specs=[
            pl.BlockSpec(memory_space=pltpu.SMEM),
            pl.BlockSpec(memory_space=pltpu.VMEM),
            pl.BlockSpec(memory_space=pltpu.VMEM),
        ],
        out_specs=pl.BlockSpec(memory_space=pltpu.VMEM),
        name="score",
    )(doc_ends, group_vectors, near_queries)
    scores = pick_scores(table, candidates, groups)
    return (vectors, scores)


def solution(mesh):
    placed = (
        P(("group", "dev"), None),
        P(),
        P("dev", None),
        P("dev", None),
        P(),
        P(),
        P(("group", "dev"), None, None),
        P("group", None),
        P(("group", "dev"), None),
    )
    return jax.shard_map(
        body,
        mesh=mesh,
        in_specs=placed,
        out_specs=(P(("group", "dev"), None), P(("group", "dev"), None)),
        check_vma=False,
    )
```

```python
import jax
import jax.numpy as jnp
from jax import lax
from jax.experimental import pallas as pl
from jax.experimental.pallas import tpu as pltpu
from jax.sharding import PartitionSpec as P

BLOCK = 256


def layer_norm(values, gain_row):
    values = values.astype(jnp.float32)
    center = jnp.mean(values, axis=-1, keepdims=True)
    spread = jnp.mean(jnp.square(values - center), axis=-1, keepdims=True)
    return (values - center) * lax.rsqrt(spread + 1e-05) * gain_row


def segment_maxima(ends_ref, vec_ref, query_rows, doc_count):
    tokens = vec_ref.shape[0]
    blocks = tokens // BLOCK
    width = query_rows.shape[0]
    row_ids = lax.broadcasted_iota(jnp.int32, (BLOCK, width), 0)
    doc_ids = lax.broadcasted_iota(jnp.int32, (doc_count, width), 0)

    def step(_, state):
        place, doc, best = state
        block = jnp.minimum(place // BLOCK, blocks - 1)
        first = pl.multiple_of(block * BLOCK, BLOCK)
        doc_end = ends_ref[doc]
        stop = jnp.minimum(doc_end, first + BLOCK)
        similar = lax.dot_general(
            vec_ref[pl.ds(first, BLOCK), :],
            query_rows,
            (((1,), (1,)), ((), ())),
            preferred_element_type=jnp.float32,
        )
        inside = (row_ids >= place - first) & (row_ids < stop - first)
        top = jnp.max(jnp.where(inside, similar, -jnp.inf), axis=0, keepdims=True)
        best = jnp.where(doc_ids == doc, jnp.maximum(best, top), best)
        doc = jnp.minimum(doc + (stop == doc_end).astype(jnp.int32), doc_count - 1)
        return stop, doc, best

    start = jnp.full((doc_count, width), -jnp.inf, jnp.float32)
    state = (jnp.int32(0), jnp.int32(0), start)
    return lax.fori_loop(0, blocks + doc_count - 1, step, state)[2]


def score_kernel(query_len, ends_ref, vec_ref, query_ref, out_ref):
    doc_count = out_ref.shape[0]
    best = segment_maxima(ends_ref, vec_ref, query_ref[...], doc_count).astype(jnp.bfloat16)
    rows = lax.broadcasted_iota(jnp.int32, (best.shape[1], out_ref.shape[1]), 0)
    cols = lax.broadcasted_iota(jnp.int32, (best.shape[1], out_ref.shape[1]), 1)
    adder = (rows // query_len == cols).astype(jnp.bfloat16)
    out_ref[...] = jnp.dot(best, adder, preferred_element_type=jnp.float32) / query_len


MESH = pl.DeviceIdType.MESH
SIDE = 4
OFFSETS = (0, -1, 1, 2)
TILE = 512


def place():
    dev = lax.axis_index("dev")
    core = dev % 2
    chip = dev // 2
    x, y = chip // SIDE, chip % SIDE

    def at(dx, dy):
        return (((x + dx + SIDE) % SIDE) * SIDE + (y + dy + SIDE) % SIDE) * 2 + core

    return dev, dev + 1 - 2 * core, 1 - 2 * core, at


def greet(targets):
    barrier = pltpu.get_barrier_semaphore()
    for target in targets:
        pl.semaphore_signal(barrier, inc=1, device_id=target, device_id_type=MESH)
    pl.semaphore_wait(barrier, len(targets))


def remote(src, dst, send_sem, recv_sem, target):
    return pltpu.make_async_remote_copy(
        src_ref=src,
        dst_ref=dst,
        send_sem=send_sem,
        recv_sem=recv_sem,
        device_id=target,
        device_id_type=MESH,
    )


def weights_kernel(
    groups, wi, wo, query, tokens, norm_gain, final_gain, proj, query_out, vec_out,
    wi_out, wo_out, normed, lifted, hidden, mixed,
    ring_send, ring_recv, pair_send, pair_recv, side_send, side_recv, late_send, late_recv, query_send, query_recv, own_sem,
):
    dev, partner, flip, at = place()
    group = lax.axis_index("group")
    depth, width = wi.shape
    half_depth = depth // 2
    odd = group % 2
    tiles = width // 128
    side = (tiles // 3) * 128
    across = (tiles - tiles // 3) * 128
    cut = (across * 3 // 7) // 128 * 128
    model = wo.shape[1]
    rows = query.shape[0]
    sent = []

    def loc(p, first, second):
        return at(first, second) if p == 0 else at(second, first)

    wo_side = model // 8
    wo_across = model // 2 - wo_side

    def aligned(first):
        return pl.multiple_of(first, 128)

    def views(origin, p, part):
        wi_cols = {
            "own": (0, width),
            "all": (aligned(odd * side), across),
            0: (aligned(odd * side), cut),
            1: (aligned(odd * side + cut), across - cut),
            "give": (aligned(odd * across), side),
            "take": (aligned((1 - odd) * across), side),
        }[part]
        base = p * (model // 2)
        wo_cols = {
            "own": (base, model // 2),
            "all": (aligned(base + odd * wo_side), wo_across),
            0: (aligned(base + odd * wo_side), 2 * wo_side),
            1: (aligned(base + odd * wo_side + 2 * wo_side), wo_across - 2 * wo_side),
            "give": (aligned(base + odd * wo_across), wo_side),
            "take": (aligned(base + (1 - odd) * wo_across), wo_side),
        }[part]
        if origin is None:
            return (
                wi.at[pl.ds(p * half_depth, half_depth), pl.ds(*wi_cols)],
                wo.at[:, pl.ds(*wo_cols)],
            )
        first = pl.multiple_of(origin * depth + p * half_depth, half_depth)
        return (
            wi_out.at[pl.ds(first, half_depth), pl.ds(*wi_cols)],
            wo_out.at[origin, :, pl.ds(*wo_cols)],
        )

    def copies(source, origin, p, half, sems_send, sems_recv, index, target):
        pairs = zip(views(source, p, half), views(origin, p, half))
        return [
            remote(src, dst, sems_send.at[index, i], sems_recv.at[index, i], target if isinstance(target, dict) else {"dev": target})
            for i, (src, dst) in enumerate(pairs)
        ]

    def ring_index(p, slot, kind):
        return (p * 5 + slot) * 4 + kind

    def start(*args):
        for copy in copies(*args):
            copy.start()
            sent.append(copy)

    def ring_start(p, slot, source, origin):
        for kind, step in ((0, 1), (1, -1)):
            target = loc(p, step, 0) if slot == 0 else loc(p, 0, step)
            start(source, origin, p, "all", ring_send, ring_recv, ring_index(p, slot, kind), target)

    def ring_pass(p, slot, kind, origin):
        step = 1 if kind == 0 else -1
        target = loc(p, step, 0) if slot == 0 else loc(p, 0, step)
        start(origin, origin, p, kind, ring_send, ring_recv, ring_index(p, slot, kind + 2), target)

    def ring_wait(p, slot, kind, origin):
        half = kind - 2 if kind >= 2 else "all"
        for copy in copies(origin, origin, p, half, ring_send, ring_recv, ring_index(p, slot, kind), partner):
            copy.wait_recv()

    def pair_index(p, first, second):
        return (p * 4 + OFFSETS.index(first)) * 4 + OFFSETS.index(second)

    def arrived(p, first, second, origin):
        index = pair_index(p, first, second)
        start(origin, origin, p, "all", pair_send, pair_recv, index, partner)
        target = {"group": (group + (1 if p == 0 else groups - 1)) % groups}
        start(origin, origin, p, "give", side_send, side_recv, index, target)

    def side_wait(first, second):
        for p in (0, 1):
            origin = loc(p, first, second)
            index = pair_index(p, first, second)
            for copy in copies(origin, origin, p, "take", side_send, side_recv, index, partner):
                copy.wait_recv()
            start(origin, origin, p, "take", late_send, late_recv, index, partner)

    others = [(group + k) % groups for k in range(1, groups)]
    greet(
        [{"dev": at(*d)} for d in ((1, 0), (-1, 0), (0, 1), (0, -1))]
        + [{"dev": partner}]
        + [{"group": other} for other in others]
    )
    for p in (0, 1):
        ring_start(p, 0, None, dev)
    for p in (0, 1):
        ring_start(p, 1, None, dev)
        start(None, dev, p, "own", pair_send, pair_recv, pair_index(p, 0, 0), partner)
    own_rows = pl.ds(pl.multiple_of(group * rows, rows), rows)
    for k, other in enumerate(others):
        copy = remote(query, query_out.at[own_rows], query_send.at[k], query_recv.at[k], {"group": other})
        copy.start()
        sent.append(copy)
    kept = [
        pltpu.make_async_copy(wi, wi_out.at[pl.ds(pl.multiple_of(dev * depth, depth), depth)], own_sem.at[0]),
        pltpu.make_async_copy(wo, wo_out.at[dev], own_sem.at[1]),
        pltpu.make_async_copy(query, query_out.at[own_rows], own_sem.at[2]),
    ]
    for copy in kept:
        copy.start()
    normed[...] = layer_norm(tokens[...], norm_gain[...]).astype(jnp.bfloat16)

    for slot, first, kind in ((2, -1, 0), (3, 1, 1)):
        for p in (0, 1):
            origin = loc(p, first, 0)
            ring_wait(p, 0, kind, origin)
            ring_pass(p, 0, kind, origin)
            ring_start(p, slot, origin, origin)
            arrived(p, first, 0, origin)
    for p in (0, 1):
        origin = loc(p, 2, 0)
        ring_wait(p, 0, 2, origin)
        ring_wait(p, 0, 3, origin)
        ring_start(p, 4, origin, origin)
        arrived(p, 2, 0, origin)
    for slot, first in ((1, 0), (2, -1), (3, 1), (4, 2)):
        for second, kind in ((-1, 0), (1, 1)):
            for p in (0, 1):
                origin = loc(p, first, second)
                ring_wait(p, slot, kind, origin)
                ring_pass(p, slot, kind, origin)
                arrived(p, first, second, origin)
        if first != 0:
            side_wait(first, 0)
    for slot, first in ((1, 0), (2, -1), (3, 1), (4, 2)):
        for p in (0, 1):
            origin = loc(p, first, 2)
            ring_wait(p, slot, 2, origin)
            ring_wait(p, slot, 3, origin)
            arrived(p, first, 2, origin)
        side_wait(first, -1)
        side_wait(first, 1)
    for first in (0, -1, 1, 2):
        side_wait(first, 2)

    for k in range(groups - 1):
        source = (group + groups - 1 - k) % groups
        landing = query_out.at[pl.ds(pl.multiple_of(source * rows, rows), rows)]
        remote(query, landing, query_send.at[k], query_recv.at[k], {"dev": partner}).wait_recv()
    for first in OFFSETS:
        for second in OFFSETS:
            for p in (0, 1):
                origin = loc(p, first, second) + flip
                index = pair_index(p, first, second)
                own = first == 0 and second == 0
                part = "own" if own else "all"
                for copy in copies(origin, origin, p, part, pair_send, pair_recv, index, partner):
                    copy.wait_recv()
                if not own:
                    for copy in copies(origin, origin, p, "take", late_send, late_recv, index, partner):
                        copy.wait_recv()
    for copy in kept:
        copy.wait()

    @pl.loop(0, width // TILE)
    def _(j):
        cols = pl.ds(pl.multiple_of(j * TILE, TILE), TILE)
        lifted[:, cols] = jnp.dot(normed[...], wi_out[:, cols], preferred_element_type=jnp.float32)

    if width % TILE:
        cols = pl.ds(width - width % TILE, width % TILE)
        lifted[:, cols] = jnp.dot(normed[...], wi_out[:, cols], preferred_element_type=jnp.float32)

    @pl.loop(0, hidden.shape[0] // 16)
    def _(i):
        strip = pl.ds(pl.multiple_of(i * 16, 16), 16)
        both = lifted[strip, :]
        gated = both[:, : width // 2]
        gelu = 0.5 * gated * (1.0 + lax.erf(gated * 0.5**0.5))
        hidden[strip, :] = (gelu * both[:, width // 2 :]).astype(jnp.bfloat16)

    mixed[...] = tokens[...].astype(jnp.float32)
    kept_rows = wo.shape[0]
    for k in range(0, wo_out.shape[0], 4):
        part = None
        for i in range(k, k + 4):
            term = jnp.dot(
                hidden[:, i * kept_rows : (i + 1) * kept_rows],
                wo_out[i],
                preferred_element_type=jnp.float32,
            )
            part = term if part is None else part + term
        mixed[...] += part
    normed_out = layer_norm(mixed[...], final_gain[...]).astype(jnp.bfloat16)
    projected = jnp.dot(normed_out, proj[...], preferred_element_type=jnp.float32)
    inverse = lax.rsqrt(jnp.sum(projected * projected, axis=-1, keepdims=True) + 1e-06)
    vec_out[...] = (projected * inverse).astype(jnp.bfloat16)
    for copy in sent:
        copy.wait_send()


def encode(wi_weight, wo_weight, query_rows, tokens, norm_gain, final_gain, proj, groups, devs):
    depth, width = wi_weight.shape
    kept_rows, model = wo_weight.shape
    rows, vector_dim = query_rows.shape
    return pl.pallas_call(
        lambda *refs: weights_kernel(groups, *refs),
        out_shape=(
            jax.ShapeDtypeStruct((groups * rows, vector_dim), query_rows.dtype),
            jax.ShapeDtypeStruct((tokens.shape[0], vector_dim), jnp.bfloat16),
        ),
        in_specs=[pl.BlockSpec(memory_space=pltpu.VMEM)] * 7,
        out_specs=[pl.BlockSpec(memory_space=pltpu.VMEM)] * 2,
        scratch_shapes=[
            pltpu.VMEM((devs * depth, width), wi_weight.dtype),
            pltpu.VMEM((devs, kept_rows, model), wo_weight.dtype),
            pltpu.VMEM(tokens.shape, jnp.bfloat16),
            pltpu.VMEM((tokens.shape[0], width), jnp.float32),
            pltpu.VMEM((tokens.shape[0], width // 2), jnp.bfloat16),
            pltpu.VMEM(tokens.shape, jnp.float32),
            pltpu.SemaphoreType.DMA((40, 2)),
            pltpu.SemaphoreType.DMA((40, 2)),
            pltpu.SemaphoreType.DMA((32, 2)),
            pltpu.SemaphoreType.DMA((32, 2)),
            pltpu.SemaphoreType.DMA((32, 2)),
            pltpu.SemaphoreType.DMA((32, 2)),
            pltpu.SemaphoreType.DMA((32, 2)),
            pltpu.SemaphoreType.DMA((32, 2)),
            pltpu.SemaphoreType.DMA((groups - 1,)),
            pltpu.SemaphoreType.DMA((groups - 1,)),
            pltpu.SemaphoreType.DMA((3,)),
        ],
        compiler_params=pltpu.CompilerParams(collective_id=0, has_side_effects=True),
        name="encode",
    )(wi_weight, wo_weight, query_rows, tokens, norm_gain, final_gain, proj)


def vectors_kernel(vec, out, send_sem, recv_sem, pair_send, pair_recv, own_sem):
    dev, partner, flip, at = place()
    rows = vec.shape[0]

    def block(origin):
        return out.at[pl.ds(pl.multiple_of(origin * rows, rows), rows)]

    steps = [(dx, dy) for dx in OFFSETS for dy in OFFSETS if (dx, dy) != (0, 0)]
    steps.sort(key=lambda d: -abs(d[0]) - abs(d[1]))
    greet([{"dev": at(dx, dy)} for dx, dy in steps] + [{"dev": partner}])
    sent = []
    for k, (dx, dy) in enumerate(steps):
        sent.append(remote(vec, block(dev), send_sem.at[k], recv_sem.at[k], {"dev": at(dx, dy)}))
        sent[-1].start()
    sent.append(remote(vec, block(dev), pair_send.at[15], pair_recv.at[15], {"dev": partner}))
    sent[-1].start()
    kept = pltpu.make_async_copy(vec, block(dev), own_sem)
    kept.start()
    for k, (dx, dy) in reversed(list(enumerate(steps))):
        origin = at(-dx, -dy)
        remote(vec, block(origin), send_sem.at[k], recv_sem.at[k], {"dev": partner}).wait_recv()
        sent.append(remote(block(origin), block(origin), pair_send.at[k], pair_recv.at[k], {"dev": partner}))
        sent[-1].start()
    for k, (dx, dy) in enumerate(steps + [(0, 0)]):
        origin = at(-dx, -dy) + flip
        remote(vec, block(origin), pair_send.at[k], pair_recv.at[k], {"dev": partner}).wait_recv()
    for copy in sent:
        copy.wait_send()
    kept.wait()


def gather_vectors(vectors, devs):
    rows, vector_dim = vectors.shape
    return pl.pallas_call(
        vectors_kernel,
        out_shape=jax.ShapeDtypeStruct((devs * rows, vector_dim), vectors.dtype),
        in_specs=[pl.BlockSpec(memory_space=pltpu.VMEM)],
        out_specs=pl.BlockSpec(memory_space=pltpu.VMEM),
        scratch_shapes=[
            pltpu.SemaphoreType.DMA((15,)),
            pltpu.SemaphoreType.DMA((15,)),
            pltpu.SemaphoreType.DMA((16,)),
            pltpu.SemaphoreType.DMA((16,)),
            pltpu.SemaphoreType.DMA,
        ],
        compiler_params=pltpu.CompilerParams(collective_id=1, has_side_effects=True),
        name="vectors",
    )(vectors)


def pick_kernel(groups, table, wanted, out, tables, send_sem, recv_sem, own_sem):
    group = lax.axis_index("group")
    others = [(group + k) % groups for k in range(1, groups)]
    greet([{"group": other} for other in others])
    sent = []
    for k, other in enumerate(others):
        sent.append(remote(table, tables.at[group], send_sem.at[k], recv_sem.at[k], {"group": other}))
        sent[-1].start()
    kept = pltpu.make_async_copy(table, tables.at[group], own_sem)
    kept.start()
    per_query, listed = wanted.shape
    docs = table.shape[0]
    for k in range(groups - 1):
        source = (group + groups - 1 - k) % groups
        remote(table, tables.at[source], send_sem.at[k], recv_sem.at[k], {"group": other}).wait_recv()
    kept.wait()
    for copy in sent:
        copy.wait_send()
    lanes = lax.broadcasted_iota(jnp.int32, (docs, table.shape[1]), 1)
    labels = lax.broadcasted_iota(jnp.int32, (docs, listed), 0)
    for q in range(per_query):
        row = wanted[pl.ds(q, 1), :]
        total = jnp.zeros((1, listed), jnp.float32)
        for g in range(groups):
            mine = jnp.where(lanes == group * per_query + q, tables[g], 0.0)
            column = jnp.sum(mine, axis=1, keepdims=True)
            hit = jnp.where(labels + g * docs == row, column, 0.0)
            total = total + jnp.sum(hit, axis=0, keepdims=True)
        out[pl.ds(q, 1), :] = total


def pick_scores(table, candidates, groups):
    return pl.pallas_call(
        lambda *refs: pick_kernel(groups, *refs),
        out_shape=jax.ShapeDtypeStruct(candidates.shape, jnp.float32),
        in_specs=[pl.BlockSpec(memory_space=pltpu.VMEM)] * 2,
        out_specs=pl.BlockSpec(memory_space=pltpu.VMEM),
        scratch_shapes=[
            pltpu.VMEM((groups,) + table.shape, jnp.float32),
            pltpu.SemaphoreType.DMA((groups - 1,)),
            pltpu.SemaphoreType.DMA((groups - 1,)),
            pltpu.SemaphoreType.DMA,
        ],
        compiler_params=pltpu.CompilerParams(collective_id=2, has_side_effects=True),
        name="pick",
    )(table, candidates)


def body(
    corpus_tokens,
    norm_gain,
    wi_weight,
    wo_weight,
    final_gain,
    proj_weight,
    query_vectors,
    doc_lengths,
    candidates,
):
    groups = lax.axis_size("group")
    doc_count = doc_lengths.shape[1]
    per_query, query_len, vector_dim = query_vectors.shape
    devs = lax.axis_size("dev")
    near_queries, vectors = encode(
        wi_weight,
        wo_weight,
        query_vectors.reshape(-1, vector_dim),
        corpus_tokens,
        norm_gain.reshape(1, -1),
        final_gain.reshape(1, -1),
        proj_weight,
        groups,
        devs,
    )
    group_vectors = gather_vectors(vectors, devs)
    doc_ends = jnp.cumsum(doc_lengths[0])
    table = pl.pallas_call(
        lambda *refs: score_kernel(query_len, *refs),
        out_shape=jax.ShapeDtypeStruct((doc_count, 128), jnp.float32),
        in_specs=[
            pl.BlockSpec(memory_space=pltpu.SMEM),
            pl.BlockSpec(memory_space=pltpu.VMEM),
            pl.BlockSpec(memory_space=pltpu.VMEM),
        ],
        out_specs=pl.BlockSpec(memory_space=pltpu.VMEM),
        name="score",
    )(doc_ends, group_vectors, near_queries)
    scores = pick_scores(table, candidates, groups)
    return (vectors, scores)


def solution(mesh):
    placed = (
        P(("group", "dev"), None),
        P(),
        P("dev", None),
        P("dev", None),
        P(),
        P(),
        P(("group", "dev"), None, None),
        P("group", None),
        P(("group", "dev"), None),
    )
    return jax.shard_map(
        body,
        mesh=mesh,
        in_specs=placed,
        out_specs=(P(("group", "dev"), None), P(("group", "dev"), None)),
        check_vma=False,
    )
```

```python
import jax
import jax.numpy as jnp
from jax import lax
from jax.experimental import pallas as pl
from jax.experimental.pallas import tpu as pltpu
from jax.sharding import PartitionSpec as P

BLOCK = 256


def layer_norm(values, gain_row):
    values = values.astype(jnp.float32)
    center = jnp.mean(values, axis=-1, keepdims=True)
    spread = jnp.mean(jnp.square(values - center), axis=-1, keepdims=True)
    return (values - center) * lax.rsqrt(spread + 1e-05) * gain_row


def segment_maxima(ends_ref, vec_ref, query_rows, doc_count):
    tokens = vec_ref.shape[0]
    blocks = tokens // BLOCK
    width = query_rows.shape[0]
    row_ids = lax.broadcasted_iota(jnp.int32, (BLOCK, 1), 0)
    doc_ids = lax.broadcasted_iota(jnp.int32, (doc_count, width), 0)

    def step(_, state):
        place, doc, best = state
        block = jnp.minimum(place // BLOCK, blocks - 1)
        first = pl.multiple_of(block * BLOCK, BLOCK)
        doc_end = ends_ref[doc]
        stop = jnp.minimum(doc_end, first + BLOCK)
        similar = lax.dot_general(
            vec_ref[pl.ds(first, BLOCK), :],
            query_rows,
            (((1,), (1,)), ((), ())),
            preferred_element_type=jnp.float32,
        )
        inside = (row_ids >= place - first) & (row_ids < stop - first)
        top = jnp.max(similar + jnp.where(inside, 0.0, -jnp.inf), axis=0, keepdims=True)
        best = jnp.where(doc_ids == doc, jnp.maximum(best, top), best)
        doc = jnp.minimum(doc + (stop == doc_end).astype(jnp.int32), doc_count - 1)
        return stop, doc, best

    start = jnp.full((doc_count, width), -jnp.inf, jnp.float32)
    state = (jnp.int32(0), jnp.int32(0), start)

    def steps(i, state):
        for _ in range(STEPS):
            state = step(i, state)
        return state

    return lax.fori_loop(0, pl.cdiv(blocks + doc_count - 1, STEPS), steps, state)[2]


def score_kernel(query_len, ends_ref, vec_ref, query_ref, out_ref):
    doc_count = out_ref.shape[0]
    best = segment_maxima(ends_ref, vec_ref, query_ref[...], doc_count).astype(jnp.bfloat16)
    rows = lax.broadcasted_iota(jnp.int32, (best.shape[1], out_ref.shape[1]), 0)
    cols = lax.broadcasted_iota(jnp.int32, (best.shape[1], out_ref.shape[1]), 1)
    adder = (rows // query_len == cols).astype(jnp.bfloat16)
    out_ref[...] = jnp.dot(best, adder, preferred_element_type=jnp.float32) / query_len


MESH = pl.DeviceIdType.MESH
SIDE = 4
OFFSETS = (0, -1, 1, 2)
TILE = 512
CROSS = (1, 2)
STEPS = 4


def place():
    dev = lax.axis_index("dev")
    core = dev % 2
    chip = dev // 2
    x, y = chip // SIDE, chip % SIDE

    def at(dx, dy):
        return (((x + dx + SIDE) % SIDE) * SIDE + (y + dy + SIDE) % SIDE) * 2 + core

    return dev, dev + 1 - 2 * core, 1 - 2 * core, at


def greet(targets):
    barrier = pltpu.get_barrier_semaphore()
    for target in targets:
        pl.semaphore_signal(barrier, inc=1, device_id=target, device_id_type=MESH)
    pl.semaphore_wait(barrier, len(targets))


def remote(src, dst, send_sem, recv_sem, target):
    return pltpu.make_async_remote_copy(
        src_ref=src,
        dst_ref=dst,
        send_sem=send_sem,
        recv_sem=recv_sem,
        device_id=target,
        device_id_type=MESH,
    )


def weights_kernel(
    groups, wi, wo, query, tokens, norm_gain, final_gain, proj, query_out, vec_out,
    wi_out, wo_out, normed, lifted, hidden, mixed,
    ring_send, ring_recv, pair_send, pair_recv, side_send, side_recv, late_send, late_recv, query_send, query_recv, own_sem,
):
    dev, partner, flip, at = place()
    group = lax.axis_index("group")
    depth, width = wi.shape
    half_depth = depth // 2
    odd = group % 2
    tiles = width // 128
    side = (tiles // 3) * 128
    across = (tiles - tiles // 3) * 128
    cut = (across * 3 // 7) // 128 * 128
    model = wo.shape[1]
    rows = query.shape[0]
    sent = []

    def loc(p, first, second):
        return at(first, second) if p == 0 else at(second, first)

    wo_side = model // 8
    wo_across = model // 2 - wo_side

    def aligned(first):
        return pl.multiple_of(first, 128)

    def views(origin, p, part):
        wi_cols = {
            "own": (0, width),
            "all": (aligned(odd * side), across),
            0: (aligned(odd * side), cut),
            1: (aligned(odd * side + cut), across - cut),
            "give": (aligned(odd * across), side),
            "take": (aligned((1 - odd) * across), side),
        }[part]
        base = p * (model // 2)
        wo_cols = {
            "own": (base, model // 2),
            "all": (aligned(base + odd * wo_side), wo_across),
            0: (aligned(base + odd * wo_side), 2 * wo_side),
            1: (aligned(base + odd * wo_side + 2 * wo_side), wo_across - 2 * wo_side),
            "give": (aligned(base + odd * wo_across), wo_side),
            "take": (aligned(base + (1 - odd) * wo_across), wo_side),
        }[part]
        if origin is None:
            return (
                wi.at[pl.ds(p * half_depth, half_depth), pl.ds(*wi_cols)],
                wo.at[:, pl.ds(*wo_cols)],
            )
        first = pl.multiple_of(origin * depth + p * half_depth, half_depth)
        return (
            wi_out.at[pl.ds(first, half_depth), pl.ds(*wi_cols)],
            wo_out.at[origin, :, pl.ds(*wo_cols)],
        )

    def copies(source, origin, p, half, sems_send, sems_recv, index, target):
        pairs = zip(views(source, p, half), views(origin, p, half))
        return [
            remote(src, dst, sems_send.at[index, i], sems_recv.at[index, i], target if isinstance(target, dict) else {"dev": target})
            for i, (src, dst) in enumerate(pairs)
        ]

    def ring_index(p, slot, kind):
        return (p * 5 + slot) * 4 + kind

    def start(*args):
        for copy in copies(*args):
            copy.start()
            sent.append(copy)

    def ring_start(p, slot, source, origin):
        for kind, step in ((0, 1), (1, -1)):
            target = loc(p, step, 0) if slot == 0 else loc(p, 0, step)
            start(source, origin, p, "all", ring_send, ring_recv, ring_index(p, slot, kind), target)

    def ring_pass(p, slot, kind, origin):
        step = 1 if kind == 0 else -1
        target = loc(p, step, 0) if slot == 0 else loc(p, 0, step)
        start(origin, origin, p, kind, ring_send, ring_recv, ring_index(p, slot, kind + 2), target)

    def ring_wait(p, slot, kind, origin):
        half = kind - 2 if kind >= 2 else "all"
        for copy in copies(origin, origin, p, half, ring_send, ring_recv, ring_index(p, slot, kind), partner):
            copy.wait_recv()

    def pair_index(p, first, second):
        return (p * 4 + OFFSETS.index(first)) * 4 + OFFSETS.index(second)

    def arrived(p, first, second, origin):
        index = pair_index(p, first, second)
        start(origin, origin, p, "all", pair_send, pair_recv, index, partner)
        target = {"group": (group + (1 if p == 0 else groups - 1)) % groups}
        start(origin, origin, p, "give", side_send, side_recv, index, target)
        if second in CROSS:
            target = {"group": (group + (1 if p == 1 else groups - 1)) % groups, "dev": partner}
            start(origin, origin, p, "give", late_send, late_recv, index, target)

    def side_wait(first, second):
        for p in (0, 1):
            origin = loc(p, first, second)
            index = pair_index(p, first, second)
            for copy in copies(origin, origin, p, "take", side_send, side_recv, index, partner):
                copy.wait_recv()
            if second not in CROSS:
                start(origin, origin, p, "take", late_send, late_recv, index, partner)

    others = [(group + k) % groups for k in range(1, groups)]
    greet(
        [{"dev": at(*d)} for d in ((1, 0), (-1, 0), (0, 1), (0, -1))]
        + [{"dev": partner}]
        + [{"group": other} for other in others]
        + [{"group": others[k], "dev": partner} for k in (0, -1)]
    )
    for p in (0, 1):
        ring_start(p, 0, None, dev)
    for p in (0, 1):
        ring_start(p, 1, None, dev)
        start(None, dev, p, "own", pair_send, pair_recv, pair_index(p, 0, 0), partner)
    own_rows = pl.ds(pl.multiple_of(group * rows, rows), rows)
    for k, other in enumerate(others):
        copy = remote(query, query_out.at[own_rows], query_send.at[k], query_recv.at[k], {"group": other})
        copy.start()
        sent.append(copy)
    kept = [
        pltpu.make_async_copy(wi, wi_out.at[pl.ds(pl.multiple_of(dev * depth, depth), depth)], own_sem.at[0]),
        pltpu.make_async_copy(wo, wo_out.at[dev], own_sem.at[1]),
        pltpu.make_async_copy(query, query_out.at[own_rows], own_sem.at[2]),
    ]
    for copy in kept:
        copy.start()
    normed[...] = layer_norm(tokens[...], norm_gain[...]).astype(jnp.bfloat16)

    for slot, first, kind in ((2, -1, 0), (3, 1, 1)):
        for p in (0, 1):
            origin = loc(p, first, 0)
            ring_wait(p, 0, kind, origin)
            ring_pass(p, 0, kind, origin)
            ring_start(p, slot, origin, origin)
            arrived(p, first, 0, origin)
    for p in (0, 1):
        origin = loc(p, 2, 0)
        ring_wait(p, 0, 2, origin)
        ring_wait(p, 0, 3, origin)
        ring_start(p, 4, origin, origin)
        arrived(p, 2, 0, origin)
    for slot, first in ((1, 0), (2, -1), (3, 1), (4, 2)):
        for second, kind in ((-1, 0), (1, 1)):
            for p in (0, 1):
                origin = loc(p, first, second)
                ring_wait(p, slot, kind, origin)
                ring_pass(p, slot, kind, origin)
                arrived(p, first, second, origin)
        if first != 0:
            side_wait(first, 0)
    for slot, first in ((1, 0), (2, -1), (3, 1), (4, 2)):
        for p in (0, 1):
            origin = loc(p, first, 2)
            ring_wait(p, slot, 2, origin)
            ring_wait(p, slot, 3, origin)
            arrived(p, first, 2, origin)
        side_wait(first, -1)
        side_wait(first, 1)
    for first in (0, -1, 1, 2):
        side_wait(first, 2)

    for k in range(groups - 1):
        source = (group + groups - 1 - k) % groups
        landing = query_out.at[pl.ds(pl.multiple_of(source * rows, rows), rows)]
        remote(query, landing, query_send.at[k], query_recv.at[k], {"dev": partner}).wait_recv()
    for first in OFFSETS:
        for second in OFFSETS:
            for p in (0, 1):
                origin = loc(p, first, second) + flip
                index = pair_index(p, first, second)
                own = first == 0 and second == 0
                part = "own" if own else "all"
                for copy in copies(origin, origin, p, part, pair_send, pair_recv, index, partner):
                    copy.wait_recv()
                if not own:
                    for copy in copies(origin, origin, p, "take", late_send, late_recv, index, partner):
                        copy.wait_recv()
    for copy in kept:
        copy.wait()

    @pl.loop(0, width // TILE)
    def _(j):
        cols = pl.ds(pl.multiple_of(j * TILE, TILE), TILE)
        lifted[:, cols] = jnp.dot(normed[...], wi_out[:, cols], preferred_element_type=jnp.float32)

    if width % TILE:
        cols = pl.ds(width - width % TILE, width % TILE)
        lifted[:, cols] = jnp.dot(normed[...], wi_out[:, cols], preferred_element_type=jnp.float32)

    @pl.loop(0, hidden.shape[0] // 16)
    def _(i):
        strip = pl.ds(pl.multiple_of(i * 16, 16), 16)
        both = lifted[strip, :]
        gated = both[:, : width // 2]
        gelu = 0.5 * gated * (1.0 + lax.erf(gated * 0.5**0.5))
        hidden[strip, :] = (gelu * both[:, width // 2 :]).astype(jnp.bfloat16)

    mixed[...] = tokens[...].astype(jnp.float32)
    kept_rows = wo.shape[0]
    for k in range(0, wo_out.shape[0], 4):
        part = None
        for i in range(k, k + 4):
            term = jnp.dot(
                hidden[:, i * kept_rows : (i + 1) * kept_rows],
                wo_out[i],
                preferred_element_type=jnp.float32,
            )
            part = term if part is None else part + term
        mixed[...] += part
    normed_out = layer_norm(mixed[...], final_gain[...]).astype(jnp.bfloat16)
    projected = jnp.dot(normed_out, proj[...], preferred_element_type=jnp.float32)
    inverse = lax.rsqrt(jnp.sum(projected * projected, axis=-1, keepdims=True) + 1e-06)
    vec_out[...] = (projected * inverse).astype(jnp.bfloat16)
    for copy in sent:
        copy.wait_send()


def encode(wi_weight, wo_weight, query_rows, tokens, norm_gain, final_gain, proj, groups, devs):
    depth, width = wi_weight.shape
    kept_rows, model = wo_weight.shape
    rows, vector_dim = query_rows.shape
    return pl.pallas_call(
        lambda *refs: weights_kernel(groups, *refs),
        out_shape=(
            jax.ShapeDtypeStruct((groups * rows, vector_dim), query_rows.dtype),
            jax.ShapeDtypeStruct((tokens.shape[0], vector_dim), jnp.bfloat16),
        ),
        in_specs=[pl.BlockSpec(memory_space=pltpu.VMEM)] * 7,
        out_specs=[pl.BlockSpec(memory_space=pltpu.VMEM)] * 2,
        scratch_shapes=[
            pltpu.VMEM((devs * depth, width), wi_weight.dtype),
            pltpu.VMEM((devs, kept_rows, model), wo_weight.dtype),
            pltpu.VMEM(tokens.shape, jnp.bfloat16),
            pltpu.VMEM((tokens.shape[0], width), jnp.float32),
            pltpu.VMEM((tokens.shape[0], width // 2), jnp.bfloat16),
            pltpu.VMEM(tokens.shape, jnp.float32),
            pltpu.SemaphoreType.DMA((40, 2)),
            pltpu.SemaphoreType.DMA((40, 2)),
            pltpu.SemaphoreType.DMA((32, 2)),
            pltpu.SemaphoreType.DMA((32, 2)),
            pltpu.SemaphoreType.DMA((32, 2)),
            pltpu.SemaphoreType.DMA((32, 2)),
            pltpu.SemaphoreType.DMA((32, 2)),
            pltpu.SemaphoreType.DMA((32, 2)),
            pltpu.SemaphoreType.DMA((groups - 1,)),
            pltpu.SemaphoreType.DMA((groups - 1,)),
            pltpu.SemaphoreType.DMA((3,)),
        ],
        compiler_params=pltpu.CompilerParams(collective_id=0, has_side_effects=True),
        name="encode",
    )(wi_weight, wo_weight, query_rows, tokens, norm_gain, final_gain, proj)


def vectors_kernel(vec, out, send_sem, recv_sem, pair_send, pair_recv, own_sem):
    dev, partner, flip, at = place()
    rows = vec.shape[0]

    def block(origin):
        return out.at[pl.ds(pl.multiple_of(origin * rows, rows), rows)]

    steps = [(dx, dy) for dx in OFFSETS for dy in OFFSETS if (dx, dy) != (0, 0)]
    steps.sort(key=lambda d: -abs(d[0]) - abs(d[1]))
    greet([{"dev": at(dx, dy)} for dx, dy in steps] + [{"dev": partner}])
    sent = []
    for k, (dx, dy) in enumerate(steps):
        sent.append(remote(vec, block(dev), send_sem.at[k], recv_sem.at[k], {"dev": at(dx, dy)}))
        sent[-1].start()
    sent.append(remote(vec, block(dev), pair_send.at[15], pair_recv.at[15], {"dev": partner}))
    sent[-1].start()
    kept = pltpu.make_async_copy(vec, block(dev), own_sem)
    kept.start()
    for k, (dx, dy) in reversed(list(enumerate(steps))):
        origin = at(-dx, -dy)
        remote(vec, block(origin), send_sem.at[k], recv_sem.at[k], {"dev": partner}).wait_recv()
        sent.append(remote(block(origin), block(origin), pair_send.at[k], pair_recv.at[k], {"dev": partner}))
        sent[-1].start()
    for k, (dx, dy) in enumerate(steps + [(0, 0)]):
        origin = at(-dx, -dy) + flip
        remote(vec, block(origin), pair_send.at[k], pair_recv.at[k], {"dev": partner}).wait_recv()
    for copy in sent:
        copy.wait_send()
    kept.wait()


def gather_vectors(vectors, devs):
    rows, vector_dim = vectors.shape
    return pl.pallas_call(
        vectors_kernel,
        out_shape=jax.ShapeDtypeStruct((devs * rows, vector_dim), vectors.dtype),
        in_specs=[pl.BlockSpec(memory_space=pltpu.VMEM)],
        out_specs=pl.BlockSpec(memory_space=pltpu.VMEM),
        scratch_shapes=[
            pltpu.SemaphoreType.DMA((15,)),
            pltpu.SemaphoreType.DMA((15,)),
            pltpu.SemaphoreType.DMA((16,)),
            pltpu.SemaphoreType.DMA((16,)),
            pltpu.SemaphoreType.DMA,
        ],
        compiler_params=pltpu.CompilerParams(collective_id=1, has_side_effects=True),
        name="vectors",
    )(vectors)


def pick_kernel(groups, table, wanted, out, tables, send_sem, recv_sem, own_sem):
    group = lax.axis_index("group")
    others = [(group + k) % groups for k in range(1, groups)]
    greet([{"group": other} for other in others])
    sent = []
    for k, other in enumerate(others):
        sent.append(remote(table, tables.at[group], send_sem.at[k], recv_sem.at[k], {"group": other}))
        sent[-1].start()
    kept = pltpu.make_async_copy(table, tables.at[group], own_sem)
    kept.start()
    per_query, listed = wanted.shape
    docs = table.shape[0]
    for k in range(groups - 1):
        source = (group + groups - 1 - k) % groups
        remote(table, tables.at[source], send_sem.at[k], recv_sem.at[k], {"group": other}).wait_recv()
    kept.wait()
    for copy in sent:
        copy.wait_send()
    lanes = lax.broadcasted_iota(jnp.int32, (docs, table.shape[1]), 1)
    labels = lax.broadcasted_iota(jnp.int32, (docs, listed), 0)
    for q in range(per_query):
        row = wanted[pl.ds(q, 1), :]
        total = jnp.zeros((1, listed), jnp.float32)
        for g in range(groups):
            mine = jnp.where(lanes == group * per_query + q, tables[g], 0.0)
            column = jnp.sum(mine, axis=1, keepdims=True)
            hit = jnp.where(labels + g * docs == row, column, 0.0)
            total = total + jnp.sum(hit, axis=0, keepdims=True)
        out[pl.ds(q, 1), :] = total


def pick_scores(table, candidates, groups):
    return pl.pallas_call(
        lambda *refs: pick_kernel(groups, *refs),
        out_shape=jax.ShapeDtypeStruct(candidates.shape, jnp.float32),
        in_specs=[pl.BlockSpec(memory_space=pltpu.VMEM)] * 2,
        out_specs=pl.BlockSpec(memory_space=pltpu.VMEM),
        scratch_shapes=[
            pltpu.VMEM((groups,) + table.shape, jnp.float32),
            pltpu.SemaphoreType.DMA((groups - 1,)),
            pltpu.SemaphoreType.DMA((groups - 1,)),
            pltpu.SemaphoreType.DMA,
        ],
        compiler_params=pltpu.CompilerParams(collective_id=2, has_side_effects=True),
        name="pick",
    )(table, candidates)


def body(
    corpus_tokens,
    norm_gain,
    wi_weight,
    wo_weight,
    final_gain,
    proj_weight,
    query_vectors,
    doc_lengths,
    candidates,
):
    groups = lax.axis_size("group")
    doc_count = doc_lengths.shape[1]
    per_query, query_len, vector_dim = query_vectors.shape
    devs = lax.axis_size("dev")
    near_queries, vectors = encode(
        wi_weight,
        wo_weight,
        query_vectors.reshape(-1, vector_dim),
        corpus_tokens,
        norm_gain.reshape(1, -1),
        final_gain.reshape(1, -1),
        proj_weight,
        groups,
        devs,
    )
    group_vectors = gather_vectors(vectors, devs)
    doc_ends = jnp.cumsum(doc_lengths[0])
    table = pl.pallas_call(
        lambda *refs: score_kernel(query_len, *refs),
        out_shape=jax.ShapeDtypeStruct((doc_count, 128), jnp.float32),
        in_specs=[
            pl.BlockSpec(memory_space=pltpu.SMEM),
            pl.BlockSpec(memory_space=pltpu.VMEM),
            pl.BlockSpec(memory_space=pltpu.VMEM),
        ],
        out_specs=pl.BlockSpec(memory_space=pltpu.VMEM),
        name="score",
    )(doc_ends, group_vectors, near_queries)
    scores = pick_scores(table, candidates, groups)
    return (vectors, scores)


def solution(mesh):
    placed = (
        P(("group", "dev"), None),
        P(),
        P("dev", None),
        P("dev", None),
        P(),
        P(),
        P(("group", "dev"), None, None),
        P("group", None),
        P(("group", "dev"), None),
    )
    return jax.shard_map(
        body,
        mesh=mesh,
        in_specs=placed,
        out_specs=(P(("group", "dev"), None), P(("group", "dev"), None)),
        check_vma=False,
    )
```

```python
import jax
import jax.numpy as jnp
from jax import lax
from jax.experimental import pallas as pl
from jax.experimental.pallas import tpu as pltpu
from jax.sharding import PartitionSpec as P

BLOCK = 256


def layer_norm(values, gain_row):
    values = values.astype(jnp.float32)
    center = jnp.mean(values, axis=-1, keepdims=True)
    spread = jnp.mean(jnp.square(values - center), axis=-1, keepdims=True)
    return (values - center) * lax.rsqrt(spread + 1e-05) * gain_row


def segment_maxima(ends_ref, vec_ref, query_rows, doc_count):
    tokens = vec_ref.shape[0]
    blocks = tokens // BLOCK
    width = query_rows.shape[0]
    row_ids = lax.broadcasted_iota(jnp.int32, (BLOCK, 1), 0)
    doc_ids = lax.broadcasted_iota(jnp.int32, (doc_count, width), 0)

    def step(_, state):
        place, doc, best = state
        block = jnp.minimum(place // BLOCK, blocks - 1)
        first = pl.multiple_of(block * BLOCK, BLOCK)
        doc_end = ends_ref[doc]
        stop = jnp.minimum(doc_end, first + BLOCK)
        similar = lax.dot_general(
            vec_ref[pl.ds(first, BLOCK), :],
            query_rows,
            (((1,), (1,)), ((), ())),
            preferred_element_type=jnp.float32,
        )
        inside = (row_ids >= place - first) & (row_ids < stop - first)
        top = jnp.max(similar + jnp.where(inside, 0.0, -jnp.inf), axis=0, keepdims=True)
        best = jnp.where(doc_ids == doc, jnp.maximum(best, top), best)
        doc = jnp.minimum(doc + (stop == doc_end).astype(jnp.int32), doc_count - 1)
        return stop, doc, best

    start = jnp.full((doc_count, width), -jnp.inf, jnp.float32)
    state = (jnp.int32(0), jnp.int32(0), start)

    def steps(i, state):
        for _ in range(STEPS):
            state = step(i, state)
        return state

    return lax.fori_loop(0, pl.cdiv(blocks + doc_count - 1, STEPS), steps, state)[2]


def score_kernel(query_len, ends_ref, vec_ref, query_ref, out_ref):
    doc_count = out_ref.shape[0]
    best = segment_maxima(ends_ref, vec_ref, query_ref[...], doc_count).astype(jnp.bfloat16)
    rows = lax.broadcasted_iota(jnp.int32, (best.shape[1], out_ref.shape[1]), 0)
    cols = lax.broadcasted_iota(jnp.int32, (best.shape[1], out_ref.shape[1]), 1)
    adder = (rows // query_len == cols).astype(jnp.bfloat16)
    out_ref[...] = jnp.dot(best, adder, preferred_element_type=jnp.float32) / query_len


MESH = pl.DeviceIdType.MESH
SIDE = 4
OFFSETS = (0, -1, 1, 2)
TILE = 512
STEPS = 4


def place():
    dev = lax.axis_index("dev")
    core = dev % 2
    chip = dev // 2
    x, y = chip // SIDE, chip % SIDE

    def at(dx, dy):
        return (((x + dx + SIDE) % SIDE) * SIDE + (y + dy + SIDE) % SIDE) * 2 + core

    return dev, dev + 1 - 2 * core, 1 - 2 * core, at


def greet(targets):
    barrier = pltpu.get_barrier_semaphore()
    for target in targets:
        pl.semaphore_signal(barrier, inc=1, device_id=target, device_id_type=MESH)
    pl.semaphore_wait(barrier, len(targets))


def remote(src, dst, send_sem, recv_sem, target):
    return pltpu.make_async_remote_copy(
        src_ref=src,
        dst_ref=dst,
        send_sem=send_sem,
        recv_sem=recv_sem,
        device_id=target,
        device_id_type=MESH,
    )


def weights_kernel(
    groups, wi, wo, query, tokens, norm_gain, final_gain, proj, query_out, vec_out,
    wi_out, wo_out, normed, lifted, hidden, mixed,
    ring_send, ring_recv, pair_send, pair_recv, query_send, query_recv, own_sem,
):
    dev, partner, flip, at = place()
    group = lax.axis_index("group")
    depth, width = wi.shape
    half_depth = depth // 2
    cut = (width // 256) * 128 + 128
    model = wo.shape[1]
    rows = query.shape[0]
    sent = []

    def loc(p, first, second):
        return at(first, second) if p == 0 else at(second, first)

    def views(origin, p, half):
        wi_cols = {None: (0, width), 0: (0, cut), 1: (cut, width - cut)}[half]
        wo_cols = (p * model // 2 + (model // 4 if half == 1 else 0), model // (2 if half is None else 4))
        if origin is None:
            return (
                wi.at[pl.ds(p * half_depth, half_depth), pl.ds(*wi_cols)],
                wo.at[:, pl.ds(*wo_cols)],
            )
        first = pl.multiple_of(origin * depth + p * half_depth, half_depth)
        return (
            wi_out.at[pl.ds(first, half_depth), pl.ds(*wi_cols)],
            wo_out.at[origin, :, pl.ds(*wo_cols)],
        )

    def copies(source, origin, p, half, sems_send, sems_recv, index, target):
        pairs = zip(views(source, p, half), views(origin, p, half))
        return [
            remote(src, dst, sems_send.at[index, i], sems_recv.at[index, i], {"dev": target})
            for i, (src, dst) in enumerate(pairs)
        ]

    def ring_index(p, slot, kind):
        return (p * 5 + slot) * 4 + kind

    def start(*args):
        for copy in copies(*args):
            copy.start()
            sent.append(copy)

    def ring_start(p, slot, source, origin):
        for kind, step in ((0, 1), (1, -1)):
            target = loc(p, step, 0) if slot == 0 else loc(p, 0, step)
            start(source, origin, p, None, ring_send, ring_recv, ring_index(p, slot, kind), target)

    def ring_pass(p, slot, kind, origin):
        step = 1 if kind == 0 else -1
        target = loc(p, step, 0) if slot == 0 else loc(p, 0, step)
        start(origin, origin, p, kind, ring_send, ring_recv, ring_index(p, slot, kind + 2), target)

    def ring_wait(p, slot, kind, origin):
        half = kind - 2 if kind >= 2 else None
        for copy in copies(origin, origin, p, half, ring_send, ring_recv, ring_index(p, slot, kind), partner):
            copy.wait_recv()

    def pair_index(p, first, second):
        return (p * 4 + OFFSETS.index(first)) * 4 + OFFSETS.index(second)

    def pair_start(p, first, second, source, origin):
        start(source, origin, p, None, pair_send, pair_recv, pair_index(p, first, second), partner)

    others = [(group + k) % groups for k in range(1, groups)]
    greet(
        [{"dev": at(*d)} for d in ((1, 0), (-1, 0), (0, 1), (0, -1))]
        + [{"dev": partner}]
        + [{"group": other} for other in others]
    )
    for p in (0, 1):
        ring_start(p, 0, None, dev)
    for p in (0, 1):
        ring_start(p, 1, None, dev)
        pair_start(p, 0, 0, None, dev)
    own_rows = pl.ds(pl.multiple_of(group * rows, rows), rows)
    for k, other in enumerate(others):
        copy = remote(query, query_out.at[own_rows], query_send.at[k], query_recv.at[k], {"group": other})
        copy.start()
        sent.append(copy)
    kept = [
        pltpu.make_async_copy(wi, wi_out.at[pl.ds(pl.multiple_of(dev * depth, depth), depth)], own_sem.at[0]),
        pltpu.make_async_copy(wo, wo_out.at[dev], own_sem.at[1]),
        pltpu.make_async_copy(query, query_out.at[own_rows], own_sem.at[2]),
    ]
    for copy in kept:
        copy.start()
    normed[...] = layer_norm(tokens[...], norm_gain[...]).astype(jnp.bfloat16)

    for slot, first, kind in ((2, -1, 0), (3, 1, 1)):
        for p in (0, 1):
            origin = loc(p, first, 0)
            ring_wait(p, 0, kind, origin)
            ring_pass(p, 0, kind, origin)
            ring_start(p, slot, origin, origin)
            pair_start(p, first, 0, origin, origin)
    for p in (0, 1):
        origin = loc(p, 2, 0)
        ring_wait(p, 0, 2, origin)
        ring_wait(p, 0, 3, origin)
        ring_start(p, 4, origin, origin)
        pair_start(p, 2, 0, origin, origin)
    for slot, first in ((1, 0), (2, -1), (3, 1), (4, 2)):
        for second, kind in ((-1, 0), (1, 1)):
            for p in (0, 1):
                origin = loc(p, first, second)
                ring_wait(p, slot, kind, origin)
                ring_pass(p, slot, kind, origin)
                pair_start(p, first, second, origin, origin)
    for slot, first in ((1, 0), (2, -1), (3, 1), (4, 2)):
        for p in (0, 1):
            origin = loc(p, first, 2)
            ring_wait(p, slot, 2, origin)
            ring_wait(p, slot, 3, origin)
            pair_start(p, first, 2, origin, origin)

    for k in range(groups - 1):
        source = (group + groups - 1 - k) % groups
        landing = query_out.at[pl.ds(pl.multiple_of(source * rows, rows), rows)]
        remote(query, landing, query_send.at[k], query_recv.at[k], {"dev": partner}).wait_recv()
    for first in OFFSETS:
        for second in OFFSETS:
            for p in (0, 1):
                origin = loc(p, first, second) + flip
                index = pair_index(p, first, second)
                for copy in copies(origin, origin, p, None, pair_send, pair_recv, index, partner):
                    copy.wait_recv()
    for copy in kept:
        copy.wait()

    @pl.loop(0, width // TILE)
    def _(j):
        cols = pl.ds(pl.multiple_of(j * TILE, TILE), TILE)
        lifted[:, cols] = jnp.dot(normed[...], wi_out[:, cols], preferred_element_type=jnp.float32)

    if width % TILE:
        cols = pl.ds(width - width % TILE, width % TILE)
        lifted[:, cols] = jnp.dot(normed[...], wi_out[:, cols], preferred_element_type=jnp.float32)

    @pl.loop(0, hidden.shape[0] // 16)
    def _(i):
        strip = pl.ds(pl.multiple_of(i * 16, 16), 16)
        both = lifted[strip, :]
        gated = both[:, : width // 2]
        gelu = 0.5 * gated * (1.0 + lax.erf(gated * 0.5**0.5))
        hidden[strip, :] = (gelu * both[:, width // 2 :]).astype(jnp.bfloat16)

    mixed[...] = tokens[...].astype(jnp.float32)
    kept_rows = wo.shape[0]
    for k in range(0, wo_out.shape[0], 4):
        part = None
        for i in range(k, k + 4):
            term = jnp.dot(
                hidden[:, i * kept_rows : (i + 1) * kept_rows],
                wo_out[i],
                preferred_element_type=jnp.float32,
            )
            part = term if part is None else part + term
        mixed[...] += part
    normed_out = layer_norm(mixed[...], final_gain[...]).astype(jnp.bfloat16)
    projected = jnp.dot(normed_out, proj[...], preferred_element_type=jnp.float32)
    inverse = lax.rsqrt(jnp.sum(projected * projected, axis=-1, keepdims=True) + 1e-06)
    vec_out[...] = (projected * inverse).astype(jnp.bfloat16)
    for copy in sent:
        copy.wait_send()


def encode(wi_weight, wo_weight, query_rows, tokens, norm_gain, final_gain, proj, groups, devs):
    depth, width = wi_weight.shape
    kept_rows, model = wo_weight.shape
    rows, vector_dim = query_rows.shape
    return pl.pallas_call(
        lambda *refs: weights_kernel(groups, *refs),
        out_shape=(
            jax.ShapeDtypeStruct((groups * rows, vector_dim), query_rows.dtype),
            jax.ShapeDtypeStruct((tokens.shape[0], vector_dim), jnp.bfloat16),
        ),
        in_specs=[pl.BlockSpec(memory_space=pltpu.VMEM)] * 7,
        out_specs=[pl.BlockSpec(memory_space=pltpu.VMEM)] * 2,
        scratch_shapes=[
            pltpu.VMEM((devs * depth, width), wi_weight.dtype),
            pltpu.VMEM((devs, kept_rows, model), wo_weight.dtype),
            pltpu.VMEM(tokens.shape, jnp.bfloat16),
            pltpu.VMEM((tokens.shape[0], width), jnp.float32),
            pltpu.VMEM((tokens.shape[0], width // 2), jnp.bfloat16),
            pltpu.VMEM(tokens.shape, jnp.float32),
            pltpu.SemaphoreType.DMA((40, 2)),
            pltpu.SemaphoreType.DMA((40, 2)),
            pltpu.SemaphoreType.DMA((32, 2)),
            pltpu.SemaphoreType.DMA((32, 2)),
            pltpu.SemaphoreType.DMA((groups - 1,)),
            pltpu.SemaphoreType.DMA((groups - 1,)),
            pltpu.SemaphoreType.DMA((3,)),
        ],
        compiler_params=pltpu.CompilerParams(collective_id=0, has_side_effects=True),
        name="encode",
    )(wi_weight, wo_weight, query_rows, tokens, norm_gain, final_gain, proj)


def vectors_kernel(vec, out, send_sem, recv_sem, pair_send, pair_recv, own_sem):
    dev, partner, flip, at = place()
    rows = vec.shape[0]

    def block(origin):
        return out.at[pl.ds(pl.multiple_of(origin * rows, rows), rows)]

    steps = [(dx, dy) for dx in OFFSETS for dy in OFFSETS if (dx, dy) != (0, 0)]
    steps.sort(key=lambda d: -abs(d[0]) - abs(d[1]))
    greet([{"dev": at(dx, dy)} for dx, dy in steps] + [{"dev": partner}])
    sent = []
    for k, (dx, dy) in enumerate(steps):
        sent.append(remote(vec, block(dev), send_sem.at[k], recv_sem.at[k], {"dev": at(dx, dy)}))
        sent[-1].start()
    sent.append(remote(vec, block(dev), pair_send.at[15], pair_recv.at[15], {"dev": partner}))
    sent[-1].start()
    kept = pltpu.make_async_copy(vec, block(dev), own_sem)
    kept.start()
    for k, (dx, dy) in reversed(list(enumerate(steps))):
        origin = at(-dx, -dy)
        remote(vec, block(origin), send_sem.at[k], recv_sem.at[k], {"dev": partner}).wait_recv()
        sent.append(remote(block(origin), block(origin), pair_send.at[k], pair_recv.at[k], {"dev": partner}))
        sent[-1].start()
    for k, (dx, dy) in enumerate(steps + [(0, 0)]):
        origin = at(-dx, -dy) + flip
        remote(vec, block(origin), pair_send.at[k], pair_recv.at[k], {"dev": partner}).wait_recv()
    for copy in sent:
        copy.wait_send()
    kept.wait()


def gather_vectors(vectors, devs):
    rows, vector_dim = vectors.shape
    return pl.pallas_call(
        vectors_kernel,
        out_shape=jax.ShapeDtypeStruct((devs * rows, vector_dim), vectors.dtype),
        in_specs=[pl.BlockSpec(memory_space=pltpu.VMEM)],
        out_specs=pl.BlockSpec(memory_space=pltpu.VMEM),
        scratch_shapes=[
            pltpu.SemaphoreType.DMA((15,)),
            pltpu.SemaphoreType.DMA((15,)),
            pltpu.SemaphoreType.DMA((16,)),
            pltpu.SemaphoreType.DMA((16,)),
            pltpu.SemaphoreType.DMA,
        ],
        compiler_params=pltpu.CompilerParams(collective_id=1, has_side_effects=True),
        name="vectors",
    )(vectors)


def pick_kernel(groups, table, wanted, out, tables, send_sem, recv_sem, own_sem):
    group = lax.axis_index("group")
    others = [(group + k) % groups for k in range(1, groups)]
    greet([{"group": other} for other in others])
    sent = []
    for k, other in enumerate(others):
        sent.append(remote(table, tables.at[group], send_sem.at[k], recv_sem.at[k], {"group": other}))
        sent[-1].start()
    kept = pltpu.make_async_copy(table, tables.at[group], own_sem)
    kept.start()
    per_query, listed = wanted.shape
    docs = table.shape[0]
    for k in range(groups - 1):
        source = (group + groups - 1 - k) % groups
        remote(table, tables.at[source], send_sem.at[k], recv_sem.at[k], {"group": other}).wait_recv()
    kept.wait()
    for copy in sent:
        copy.wait_send()
    lanes = lax.broadcasted_iota(jnp.int32, (docs, table.shape[1]), 1)
    labels = lax.broadcasted_iota(jnp.int32, (docs, listed), 0)
    for q in range(per_query):
        row = wanted[pl.ds(q, 1), :]
        total = jnp.zeros((1, listed), jnp.float32)
        for g in range(groups):
            mine = jnp.where(lanes == group * per_query + q, tables[g], 0.0)
            column = jnp.sum(mine, axis=1, keepdims=True)
            hit = jnp.where(labels + g * docs == row, column, 0.0)
            total = total + jnp.sum(hit, axis=0, keepdims=True)
        out[pl.ds(q, 1), :] = total


def pick_scores(table, candidates, groups):
    return pl.pallas_call(
        lambda *refs: pick_kernel(groups, *refs),
        out_shape=jax.ShapeDtypeStruct(candidates.shape, jnp.float32),
        in_specs=[pl.BlockSpec(memory_space=pltpu.VMEM)] * 2,
        out_specs=pl.BlockSpec(memory_space=pltpu.VMEM),
        scratch_shapes=[
            pltpu.VMEM((groups,) + table.shape, jnp.float32),
            pltpu.SemaphoreType.DMA((groups - 1,)),
            pltpu.SemaphoreType.DMA((groups - 1,)),
            pltpu.SemaphoreType.DMA,
        ],
        compiler_params=pltpu.CompilerParams(collective_id=2, has_side_effects=True),
        name="pick",
    )(table, candidates)


def body(
    corpus_tokens,
    norm_gain,
    wi_weight,
    wo_weight,
    final_gain,
    proj_weight,
    query_vectors,
    doc_lengths,
    candidates,
):
    groups = lax.axis_size("group")
    doc_count = doc_lengths.shape[1]
    per_query, query_len, vector_dim = query_vectors.shape
    devs = lax.axis_size("dev")
    near_queries, vectors = encode(
        wi_weight,
        wo_weight,
        query_vectors.reshape(-1, vector_dim),
        corpus_tokens,
        norm_gain.reshape(1, -1),
        final_gain.reshape(1, -1),
        proj_weight,
        groups,
        devs,
    )
    group_vectors = gather_vectors(vectors, devs)
    doc_ends = jnp.cumsum(doc_lengths[0])
    table = pl.pallas_call(
        lambda *refs: score_kernel(query_len, *refs),
        out_shape=jax.ShapeDtypeStruct((doc_count, 128), jnp.float32),
        in_specs=[
            pl.BlockSpec(memory_space=pltpu.SMEM),
            pl.BlockSpec(memory_space=pltpu.VMEM),
            pl.BlockSpec(memory_space=pltpu.VMEM),
        ],
        out_specs=pl.BlockSpec(memory_space=pltpu.VMEM),
        name="score",
    )(doc_ends, group_vectors, near_queries)
    scores = pick_scores(table, candidates, groups)
    return (vectors, scores)


def solution(mesh):
    placed = (
        P(("group", "dev"), None),
        P(),
        P("dev", None),
        P("dev", None),
        P(),
        P(),
        P(("group", "dev"), None, None),
        P("group", None),
        P(("group", "dev"), None),
    )
    return jax.shard_map(
        body,
        mesh=mesh,
        in_specs=placed,
        out_specs=(P(("group", "dev"), None), P(("group", "dev"), None)),
        check_vma=False,
    )
```
